256 devices in a mesh: dp: 16 (over y_hi, z), lon: 16 (over x, y_lo, core).
Axes of the slice: x: 4, y: 4 (y_hi: 2, y_lo: 2; y = y_hi * 2 + y_lo), z: 8, core: 2. Of those that a mesh axis runs over, the one named last changes fastest.
Arguments:
- fields: bfloat16 [16, 16, 2048, 192], P('dp', None, 'lon'), may hold values from -6 to 6
- cotangent: bfloat16 [16, 16, 2048, 192], P('dp', None, 'lon'), may hold values from -6 to 6
- land_sea: int32 [16, 2048], P(None, 'lon'), may hold values 0 or 1
- kernel: float32 [7, 7, 192], replicated, may hold values from -0.875 to 0.875
- ln_gain: float32 [192], replicated, may hold values from 0.5 to 1.5
- weight_in: bfloat16 [192, 768], replicated, may hold values from -0.4375 to 0.4375
- bias_in: float32 [768], replicated, may hold values from -3 to 3
- weight_out: bfloat16 [768, 192], replicated, may hold values from -0.21875 to 0.21875
Outputs:
- output: bfloat16 [16, 16, 2048, 192], P('dp', None, 'lon')
- grad_fields: bfloat16 [16, 16, 2048, 192], P('dp', None, 'lon')
- grad_in: float32 [192, 768], P('dp')
- grad_out: float32 [768, 192], P('dp')
- grad_kernel: float32 [7, 7, 192], replicated
- grad_gain: float32 [192], replicated
- grad_bias: float32 [768], replicated
The draws below stay inside these ranges and needn't reach their ends.
All inputs are finite; a program needn't handle non-finite values. No bound on the sum of `land_sea` on one device may be relied on, other than what follows from the above.
Results may differ from the reference program's by a relative error of at most 0.025.
Values may be sent and summed in bfloat16 or wider, within the bound.
A program may use at most 64 MiB of HBM per device.

```python
import math
import jax
import jax.numpy as jnp
from jax import lax

C = 192
HID = 768
KS = 7
LAT = 16
SAMPLES = 16
LON = 2048


def touch_ends(values, key, least, high):
    extent = values.shape
    place = [jax.random.randint(jax.random.fold_in(key, axis), (), 0, extent[axis]) for axis in range(len(extent))]
    values = values.at[tuple(place)].set(least)
    longest = extent.index(max(extent))
    place[longest] = (place[longest] + 1) % extent[longest]
    return values.at[tuple(place)].set(high)


def block_scale(rng, dims, pieces, smallest, largest):
    factor_of, own = 1.0, jax.random.fold_in(rng, 6)
    for dim, parts in pieces:
        steps = jnp.exp(jax.random.uniform(jax.random.fold_in(own, dim), (parts,), jnp.float32, smallest / len(pieces), largest / len(pieces)))
        factor_of = factor_of * jnp.repeat(steps, dims[dim] // parts).reshape([-1 if axis == dim else 1 for axis in range(len(dims))])
    return factor_of


def gaussian(key, dims, scale, most, split=(), dtype=jnp.bfloat16):
    drawn = scale * jax.random.normal(key, dims, jnp.float32)
    if split:
        drawn = drawn * block_scale(key, dims, split, -0.22, 0.18)
    return jnp.clip(drawn, -most, most).astype(dtype)


def setup_inputs(seed: int = 0) -> dict:
    keys = jax.random.split(jax.random.key(seed), 9)
    return {
        "fields": gaussian(keys[0], (SAMPLES, LAT, LON, C), 1.0, 6.0, ((0, 16), (2, 16))),
        "cotangent": gaussian(keys[1], (SAMPLES, LAT, LON, C), 1.0, 6.0, ((0, 16), (2, 16))),
        "land_sea": touch_ends((jax.random.randint(keys[2], (LAT, LON), 0, 4) < 3).astype(jnp.int32), jax.random.fold_in(keys[2], 1), 0, 1),
        "kernel": gaussian(keys[3], (KS, KS, C), (KS * KS) ** -0.5, 0.875, (), jnp.float32),
        "ln_gain": jnp.clip(1.0 + 0.1 * jax.random.normal(keys[4], (C,), jnp.float32), 0.5, 1.5),
        "weight_in": gaussian(keys[5], (C, HID), C ** -0.5, 0.4375),
        "bias_in": gaussian(keys[6], (HID,), 0.5, 3.0, (), jnp.float32),
        "weight_out": gaussian(keys[7], (HID, C), HID ** -0.5, 0.21875),
    }


def gelu_exact(value):
    return value * (1.0 + lax.erf(value / math.sqrt(2.0))) / 2.0

def gelu_slope(value):
    return (1.0 + lax.erf(value / math.sqrt(2.0))) / 2.0 + value * jnp.exp(-value * value / 2.0) / math.sqrt(2.0 * math.pi)

def pad_band(block):
    wrapped = jnp.concatenate([block[:, :, -3:], block, block[:, :, :3]], axis=2)
    return jnp.pad(wrapped, ((0, 0), (3, 3), (0, 0), (0, 0)))

def depthwise(padded, kernel, lat_rows, lon_cols):
    total = jnp.zeros((padded.shape[0], lat_rows, lon_cols, padded.shape[3]), jnp.float32)
    for row_off in range(7):
        for col_off in range(7):
            total = total + padded[:, row_off:row_off + lat_rows, col_off:col_off + lon_cols].astype(jnp.float32) * kernel[row_off, col_off]
    return total

def transposed(padded, kernel, lat_rows, lon_cols):
    total = jnp.zeros((padded.shape[0], lat_rows, lon_cols, padded.shape[3]), jnp.float32)
    for row_off in range(7):
        for col_off in range(7):
            total = total + padded[:, 6 - row_off:6 - row_off + lat_rows, 6 - col_off:6 - col_off + lon_cols].astype(jnp.float32) * kernel[row_off, col_off]
    return total

def kernel_terms(padded, d_conv, lat_rows, lon_cols):
    d_float = d_conv.astype(jnp.float32)
    rows_out = []
    for row_off in range(7):
        cols_out = []
        for col_off in range(7):
            window = padded[:, row_off:row_off + lat_rows, col_off:col_off + lon_cols].astype(jnp.float32)
            cols_out.append(lax.optimization_barrier(jnp.sum(window * d_float, axis=(0, 1, 2))))
        rows_out.append(jnp.stack(cols_out, axis=0))
    return jnp.stack(rows_out, axis=0)

def one_pass(fields, cotangent, mask_b, kernel, ln_gain, weight_in, bias_in, weight_out, lat_rows, lon_cols):
    channels = fields.shape[3]
    masked = fields * mask_b
    padded = pad_band(masked)
    conv = depthwise(padded, kernel, lat_rows, lon_cols)
    mean_c = lax.optimization_barrier(jnp.mean(conv, axis=-1, keepdims=True))
    centered = conv - mean_c
    inv_sigma = lax.rsqrt(lax.optimization_barrier(jnp.mean(centered * centered, axis=-1, keepdims=True)) + 1e-06)
    nhat = centered * inv_sigma
    normed = (nhat * ln_gain).astype(jnp.bfloat16)
    flat = normed.reshape(-1, channels)
    pre = jnp.dot(flat, weight_in, preferred_element_type=jnp.float32) + bias_in
    act = gelu_exact(pre).astype(jnp.bfloat16)
    branch = jnp.dot(act, weight_out, preferred_element_type=jnp.float32).reshape(fields.shape)
    mask_f = mask_b.astype(jnp.float32)
    output = (mask_f * (fields.astype(jnp.float32) + branch)).astype(jnp.bfloat16)
    grad_m = cotangent * mask_b
    grad_flat = grad_m.reshape(-1, channels)
    d_act = lax.dot_general(grad_flat, weight_out, (((1,), (1,)), ((), ())), preferred_element_type=jnp.float32)
    d_pre = (d_act * gelu_slope(pre)).astype(jnp.bfloat16)
    part_out = lax.dot_general(act, grad_flat, (((0,), (0,)), ((), ())), preferred_element_type=jnp.float32)
    part_in = lax.dot_general(flat, d_pre, (((0,), (0,)), ((), ())), preferred_element_type=jnp.float32)
    part_bias = lax.optimization_barrier(jnp.sum(d_pre.astype(jnp.float32), axis=0))
    d_normed = lax.dot_general(d_pre, weight_in, (((1,), (1,)), ((), ())), preferred_element_type=jnp.float32).reshape(conv.shape)
    part_gain = lax.optimization_barrier(jnp.sum(d_normed * nhat, axis=(0, 1, 2)))
    d_hat = d_normed * ln_gain
    d_conv = (inv_sigma * (d_hat - lax.optimization_barrier(jnp.mean(d_hat, axis=-1, keepdims=True)) - nhat * lax.optimization_barrier(jnp.mean(d_hat * nhat, axis=-1, keepdims=True)))).astype(jnp.bfloat16)
    part_kernel = kernel_terms(padded, d_conv, lat_rows, lon_cols)
    spread = transposed(pad_band(d_conv), kernel, lat_rows, lon_cols)
    grad_fields = (grad_m.astype(jnp.float32) + mask_f * spread).astype(jnp.bfloat16)
    return (output, grad_fields, part_in, part_out, part_kernel, part_gain, part_bias)

def reference(fields, cotangent, land_sea, kernel, ln_gain, weight_in, bias_in, weight_out):
    samples, lat_rows, lon_cols, channels = fields.shape
    hidden = weight_in.shape[1]
    mask_b = land_sea.astype(jnp.bfloat16)[None, :, :, None]

    def step(carry, pair):
        one_field, one_cot = pair
        results = one_pass(one_field[None], one_cot[None], mask_b, kernel, ln_gain, weight_in, bias_in, weight_out, lat_rows, lon_cols)
        carry = tuple((total + part for total, part in zip(carry, results[2:])))
        return (carry, (results[0][0], results[1][0]))
    start = (jnp.zeros((channels, hidden), jnp.float32), jnp.zeros((hidden, channels), jnp.float32), jnp.zeros((7, 7, channels), jnp.float32), jnp.zeros((channels,), jnp.float32), jnp.zeros((hidden,), jnp.float32))
    sums, stacked = lax.scan(step, start, (fields, cotangent))
    scale = 1.0 / math.sqrt(samples * lat_rows * lon_cols)
    return (stacked[0], stacked[1], sums[0] * scale, sums[1] * scale, sums[2] * scale, sums[3] * scale, sums[4] * scale)
```

```python
import functools
import math

import jax
import jax.numpy as jnp
from jax import lax
from jax.experimental import pallas as pl
from jax.experimental.pallas import tpu as pltpu
from jax.sharding import PartitionSpec as P

F32 = jnp.float32
BF16 = jnp.bfloat16
MESH = pl.DeviceIdType.MESH
ROWS = 16
CH = 192
HID = 768
LANES = 128
TILES = CH // 8
PEERS = 16
VMEM_BYTES = 60 * 1024 * 1024


def lane_ids(shape):
    return lax.broadcasted_iota(jnp.int32, shape, 1)


def pack_edges(row_of):
    group = ((lane_ids((CH, LANES)) + 4) // 8) % ROWS
    packed = jnp.zeros((CH, LANES), F32)
    for i in range(ROWS):
        row = row_of(i)
        if i:
            row = pltpu.roll(row, 8 * i, axis=1)
        packed = jnp.where(group == i, row, packed)
    return packed


def merge_edges(from_left, from_right):
    low = lane_ids((CH, LANES)) % 8 < 4
    return jnp.where(low, from_right.astype(F32), from_left.astype(F32))


def spread_edges(edges, halo_ref):
    for i in range(ROWS):
        halo_ref[i] = pltpu.roll(edges, (LANES - 8 * i) % LANES, axis=1) if i else edges


def shifted_rows(src, halo, c0, shift):
    lane = lane_ids((8, LANES))
    rows = []
    for r in range(ROWS):
        row = src[r, pl.ds(c0, 8), :]
        if shift > 0:
            row = jnp.where(lane < shift, halo[r, pl.ds(c0, 8), :], row)
        elif shift < 0:
            row = jnp.where(lane >= LANES + shift, halo[r, pl.ds(c0, 8), :], row)
        if shift:
            row = pltpu.roll(row, (LANES - shift) % LANES, axis=1)
        rows.append(row)
    return rows


def conv_tile(src, halo, taps, dst, tile, sign):
    c0 = pl.multiple_of(tile * 8, 8)
    weights = taps[pl.ds(c0, 8), :]
    total = [None] * ROWS
    for b in range(7):
        rows = shifted_rows(src, halo, c0, sign * (b - 3))
        for a in range(7):
            col = 8 * a + b
            w = jnp.broadcast_to(weights[:, col : col + 1], (8, LANES))
            for i in range(ROWS):
                r = i + sign * (a - 3)
                if 0 <= r < ROWS:
                    term = w * rows[r]
                    total[i] = term if total[i] is None else total[i] + term
    for i in range(ROWS):
        dst[i, pl.ds(c0, 8), :] = total[i]


def kernel_grad_tile(src, halo, grad, dst, tile):
    c0 = pl.multiple_of(tile * 8, 8)
    lane = lane_ids((8, LANES))
    out = jnp.zeros((8, LANES), F32)
    for b in range(7):
        rows = shifted_rows(src, halo, c0, b - 3)
        sums = [None] * 7
        for i in range(ROWS):
            g = grad[i, pl.ds(c0, 8), :]
            for a in range(7):
                r = i + a - 3
                if 0 <= r < ROWS:
                    term = g * rows[r]
                    sums[a] = term if sums[a] is None else sums[a] + term
        for a in range(7):
            col = jnp.sum(sums[a], axis=1, keepdims=True)
            out = jnp.where(lane == 8 * a + b, col, out)
    dst[pl.ds(c0, 8), :] = out


def load_taps(kern_ref, stage, taps):
    stage[...] = jnp.zeros_like(stage)
    for a in range(7):
        stage[8 * a : 8 * a + 7, :] = kern_ref[a]
    taps[...] = jnp.transpose(stage[...])


def ring_neighbours():
    me = lax.axis_index("lon")
    return lax.rem(me + PEERS - 1, PEERS), lax.rem(me + 1, PEERS)


def lon_device(lon):
    return (lax.axis_index("dp"), lon)


def edge_kernel(fields, mask, edges, mine, slots, send, recv):
    left, right = ring_neighbours()
    barrier = pltpu.get_barrier_semaphore()
    for peer in (left, right):
        pl.semaphore_signal(barrier, inc=1, device_id=lon_device(peer), device_id_type=MESH)
    maskf = mask[...].astype(F32)
    packed = pack_edges(lambda i: fields[i].astype(F32) * maskf[i : i + 1, :])
    mine[...] = packed.astype(BF16)
    pl.semaphore_wait(barrier, 2)
    copies = []
    for k, peer in enumerate((left, right)):
        copy = pltpu.make_async_remote_copy(
            src_ref=mine,
            dst_ref=slots.at[k],
            send_sem=send.at[k],
            recv_sem=recv.at[k],
            device_id=lon_device(peer),
            device_id_type=MESH,
        )
        copy.start()
        copies.append(copy)
    for copy in copies:
        copy.wait()
    edges[...] = merge_edges(slots[1], slots[0]).astype(BF16)


def gelu_terms(z):
    half = 0.5 * (1.0 + lax.erf(z * (1.0 / math.sqrt(2.0))))
    slope = half + z * (jnp.exp(z * z * -0.5) * (1.0 / math.sqrt(2.0 * math.pi)))
    return z * half, slope


def block_kernel(
    fields, cot, mask, edges, kern, gain_row, w_in, bias_row, w_out_t,
    out, d_conv, d_edges, parts,
    masked, halo, conv, stage, taps, m3, gain_col, bias_col, w_in_t, w_out, aug,
    part_in, part_out, gain_sum, blocks,
):
    maskf = mask[...].astype(F32)
    for i in range(ROWS):
        m3[i] = maskf[i : i + 1, :]
        masked[i] = fields[i].astype(F32) * maskf[i : i + 1, :]
    spread_edges(edges[...].astype(F32), halo)
    load_taps(kern, stage, taps)
    gain_col[...] = jnp.transpose(jnp.broadcast_to(gain_row[...], (LANES, CH)))
    bias_col[...] = jnp.transpose(jnp.broadcast_to(bias_row[...], (LANES, HID)))
    w_in_t[...] = jnp.transpose(w_in[...].astype(F32)).astype(BF16)
    w_out[...] = jnp.transpose(w_out_t[...].astype(F32)).astype(BF16)
    part_in[...] = jnp.zeros_like(part_in)
    part_out[...] = jnp.zeros_like(part_out)
    gain_sum[...] = jnp.zeros_like(gain_sum)
    first = lax.broadcasted_iota(jnp.int32, (16, 2 * LANES), 0) == 0
    aug[CH : CH + 16, :] = jnp.where(first, 1.0, 0.0).astype(BF16)

    def conv_step(tile, carry):
        conv_tile(masked, halo, taps, conv, tile, 1)
        return carry

    lax.fori_loop(0, TILES, conv_step, 0)

    def pair(ref, k):
        return jnp.concatenate(
            [ref[2 * k].astype(F32), ref[2 * k + 1].astype(F32)], axis=1
        )

    def chunk(k, carry):
        c = pair(conv, k)
        mu = jnp.sum(c, axis=0, keepdims=True) * (1.0 / CH)
        centered = c - mu
        var = jnp.sum(centered * centered, axis=0, keepdims=True) * (1.0 / CH)
        inv = lax.rsqrt(var + 1e-6)
        nhat = centered * inv
        gain2 = jnp.concatenate([gain_col[...], gain_col[...]], axis=1)
        aug[0:CH, :] = (nhat * gain2).astype(BF16)
        m2 = pair(m3, k)
        gm = (pair(cot, k) * m2).astype(BF16)
        branch = jnp.zeros((CH, 2 * LANES), F32)
        d_normed = jnp.zeros((CH, 2 * LANES), F32)
        for h in range(3):
            hs = slice(256 * h, 256 * h + 256)
            bias2 = jnp.concatenate([bias_col[hs, :], bias_col[hs, :]], axis=1)
            pre = jnp.dot(w_in_t[hs, :], aug[0:CH, :], preferred_element_type=F32) + bias2
            d_act = jnp.dot(w_out[hs, :], gm, preferred_element_type=F32)
            act, slope = gelu_terms(pre)
            act = act.astype(BF16)
            d_pre = (d_act * slope).astype(BF16)
            branch = branch + jnp.dot(w_out_t[:, hs], act, preferred_element_type=F32)
            d_normed = d_normed + jnp.dot(w_in[:, hs], d_pre, preferred_element_type=F32)
            part_in[:, hs] += lax.dot_general(
                aug[...], d_pre, (((1,), (1,)), ((), ())), preferred_element_type=F32
            )
            part_out[hs, :] += lax.dot_general(
                act, gm, (((1,), (1,)), ((), ())), preferred_element_type=F32
            )
        result = (m2 * (pair(fields, k) + branch)).astype(BF16)
        out[2 * k] = result[:, :LANES]
        out[2 * k + 1] = result[:, LANES:]
        along = d_normed * nhat
        gain_sum[...] += along[:, :LANES] + along[:, LANES:]
        d_hat = d_normed * gain2
        mean_d = jnp.sum(d_hat, axis=0, keepdims=True) * (1.0 / CH)
        mean_dn = jnp.sum(d_hat * nhat, axis=0, keepdims=True) * (1.0 / CH)
        d = (inv * (d_hat - mean_d - nhat * mean_dn)).astype(BF16)
        d_conv[2 * k] = d[:, :LANES]
        d_conv[2 * k + 1] = d[:, LANES:]
        return carry

    lax.fori_loop(0, ROWS // 2, chunk, 0)

    d_edges[...] = pack_edges(lambda i: d_conv[i].astype(F32)).astype(BF16)
    gain_total = jnp.sum(jnp.transpose(gain_sum[...]), axis=0, keepdims=True)
    blocks[...] = jnp.zeros_like(blocks)
    for d in range(PEERS):
        for g in range(3):
            lanes = slice(256 * g, 256 * g + 256)
            blocks[16 * g : 16 * g + 12, :] = part_in[12 * d : 12 * d + 12, lanes]
            blocks[16 * g + 12 : 16 * g + 13, :] = part_in[CH : CH + 1, lanes]
        blocks[13:14, 0:CH] = gain_total
        parts[0, d] = blocks[...].astype(BF16)
    for d in range(PEERS):
        parts[1, d, :, 0:CH] = part_out[48 * d : 48 * d + 48, :].astype(BF16)
        parts[1, d, :, CH:256] = jnp.zeros((48, 64), BF16)


def grad_kernel(
    fields, cot, mask, edges, kern, d_conv, d_edges, parts,
    grad_fields, g_in, g_out, g_gain, g_bias, g_kern,
    masked, m_halo, grad, d_halo, spread, stage, taps, taps_grad, small,
    d_slots, sib_in, half_sum, dp_in, dp_sum, lon_in, total, sib_total,
    k_pieces, k_lon, k_sum, k_dp, k_full, k_all,
    nb_send, nb_recv, one_send, one_recv, dp_send, dp_recv, lon_send, lon_recv,
    ks_send, ks_recv, kd_send, kd_recv, kg_send, kg_recv,
    *, scale
):
    dp, lon = lax.axis_index("dp"), lax.axis_index("lon")
    left, right = ring_neighbours()
    core = lax.rem(lon, 2)
    sibling = lon + 1 - 2 * core
    barrier = pltpu.get_barrier_semaphore()

    def dp_peer(k):
        return (lax.rem(dp + k, PEERS), lon)

    def lon_peer(k):
        return (dp, lax.rem(lon + k, PEERS))

    def greet(k, carry):
        pl.semaphore_signal(barrier, inc=1, device_id=dp_peer(k), device_id_type=MESH)
        pl.semaphore_signal(barrier, inc=1, device_id=lon_peer(k), device_id_type=MESH)
        return carry

    lax.fori_loop(1, PEERS, greet, 0)

    def remote(src, dst, send, recv, device):
        return pltpu.make_async_remote_copy(
            src_ref=src, dst_ref=dst, send_sem=send, recv_sem=recv,
            device_id=device, device_id_type=MESH,
        )

    def to_sibling():
        return remote(
            parts.at[1 - core], sib_in, one_send.at[0], one_recv.at[0], lon_device(sibling)
        )

    def to_neighbour(k):
        peer = (left, right)[k]
        return remote(d_edges, d_slots.at[k], nb_send.at[k], nb_recv.at[k], lon_device(peer))

    def over_dp(k):
        return remote(
            half_sum.at[lax.rem(dp + k, PEERS)], dp_in.at[k], dp_send.at[k], dp_recv.at[k],
            dp_peer(k),
        )

    def over_lon(k):
        return remote(dp_sum, lon_in.at[k], lon_send.at[k], lon_recv.at[k], lon_peer(2 * k))

    def last_sibling():
        return remote(total, sib_total, one_send.at[1], one_recv.at[1], lon_device(sibling))

    def kernel_scatter(k):
        return remote(
            k_pieces.at[lax.rem(lon + k, PEERS)], k_lon.at[k], ks_send.at[k], ks_recv.at[k],
            lon_peer(k),
        )

    def kernel_over_dp(k):
        return remote(k_sum, k_dp.at[k], kd_send.at[k], kd_recv.at[k], dp_peer(k))

    def kernel_gather(k):
        return remote(k_full, k_all.at[k], kg_send.at[k], kg_recv.at[k], lon_peer(k))

    def start_all(make, count):
        def body(k, carry):
            make(k).start()
            return carry

        lax.fori_loop(1, count, body, 0)

    def wait_all(make, count):
        def body(k, carry):
            make(k).wait()
            return carry

        lax.fori_loop(1, count, body, 0)

    def sum_slots(own, slots, count):
        def body(k, acc):
            return acc + slots[k].astype(F32)

        return lax.fori_loop(1, count, body, own.astype(F32))

    def tiles(step, lo, hi):
        def body(t, carry):
            step(t)
            return carry

        lax.fori_loop(lo, hi, body, 0)

    pl.semaphore_wait(barrier, 2 * (PEERS - 1))
    for k in range(2):
        to_neighbour(k).start()
    to_sibling().start()

    maskf = mask[...].astype(F32)
    for i in range(ROWS):
        masked[i] = fields[i].astype(F32) * maskf[i : i + 1, :]
        grad[i] = d_conv[i].astype(F32)
    spread_edges(edges[...].astype(F32), m_halo)
    load_taps(kern, stage, taps)

    def kernel_step(t):
        kernel_grad_tile(masked, m_halo, grad, taps_grad, t)

    def spread_step(t):
        conv_tile(grad, d_halo, taps, spread, t, -1)

    tiles(kernel_step, 0, 8)
    to_sibling().wait()

    def add_half(d, carry):
        half_sum[d] = (parts[core, d].astype(F32) + sib_in[d].astype(F32)).astype(BF16)
        return carry

    lax.fori_loop(0, PEERS, add_half, 0)
    start_all(over_dp, PEERS)
    tiles(kernel_step, 8, TILES)

    flipped = jnp.transpose(taps_grad[...])
    for p in range(PEERS):
        k_pieces[p] = flipped[4 * p : 4 * p + 4, :]
    start_all(kernel_scatter, PEERS)

    for k in range(2):
        to_neighbour(k).wait()
    spread_edges(merge_edges(d_slots[1], d_slots[0]), d_halo)
    tiles(spread_step, 0, 8)

    wait_all(kernel_scatter, PEERS)
    k_sum[...] = sum_slots(k_pieces[lon], k_lon, PEERS)
    start_all(kernel_over_dp, PEERS)
    tiles(spread_step, 8, 16)

    wait_all(over_dp, PEERS)
    dp_sum[...] = sum_slots(half_sum[dp], dp_in, PEERS).astype(BF16)
    start_all(over_lon, PEERS // 2)
    wait_all(kernel_over_dp, PEERS)
    k_full[...] = sum_slots(k_sum[...], k_dp, PEERS)
    start_all(kernel_gather, PEERS)
    tiles(spread_step, 16, TILES)

    wait_all(over_lon, PEERS // 2)
    total[...] = sum_slots(dp_sum[...], lon_in, PEERS // 2)
    last_sibling().start()

    for i in range(ROWS):
        m = maskf[i : i + 1, :]
        grad_fields[i] = (m * (cot[i].astype(F32) + spread[i])).astype(BF16)

    wait_all(kernel_gather, PEERS)
    k_all[0] = k_full[...]
    for p in range(PEERS):
        small[4 * p : 4 * p + 4, :] = k_all[lax.rem(lon - p + PEERS, PEERS)]
    for a in range(7):
        g_kern[a] = small[8 * a : 8 * a + 7, :] * scale

    last_sibling().wait()
    mine, other = total[...] * scale, sib_total[...] * scale
    even = core == 0
    first = jnp.where(even, mine, other)
    second = jnp.where(even, other, mine)
    for g in range(3):
        lanes = slice(256 * g, 256 * g + 256)
        g_in[:, lanes] = first[16 * g : 16 * g + 12, :]
        g_bias[:, lanes] = first[16 * g + 12 : 16 * g + 13, :]
    g_gain[...] = first[13:14, 0:CH]
    g_out[...] = second[:, 0:CH]


def vmem():
    return pl.BlockSpec(memory_space=pltpu.VMEM)


def per_device(fields, cotangent, land_sea, kernel, ln_gain, weight_in, bias_in, weight_out):
    x = jnp.transpose(fields, (0, 1, 3, 2)).reshape(ROWS, CH, LANES)
    cot = jnp.transpose(cotangent, (0, 1, 3, 2)).reshape(ROWS, CH, LANES)
    w_out_t = jnp.transpose(weight_out)
    gain_row = ln_gain.reshape(1, CH)
    bias_row = bias_in.reshape(1, HID)
    dma = pltpu.SemaphoreType.DMA
    big = (ROWS, CH, LANES)

    edges = pl.pallas_call(
        edge_kernel,
        name="field_edges",
        out_shape=jax.ShapeDtypeStruct((CH, LANES), BF16),
        in_specs=[vmem()] * 2,
        out_specs=vmem(),
        scratch_shapes=[
            pltpu.VMEM((CH, LANES), BF16),
            pltpu.VMEM((2, CH, LANES), BF16),
            dma((2,)),
            dma((2,)),
        ],
        compiler_params=pltpu.CompilerParams(
            collective_id=0, has_side_effects=True, vmem_limit_bytes=VMEM_BYTES
        ),
    )(x, land_sea)

    out, d_conv, d_edges, parts = pl.pallas_call(
        block_kernel,
        name="block",
        out_shape=(
            jax.ShapeDtypeStruct(big, BF16),
            jax.ShapeDtypeStruct(big, BF16),
            jax.ShapeDtypeStruct((CH, LANES), BF16),
            jax.ShapeDtypeStruct((2, PEERS, 48, 256), BF16),
        ),
        in_specs=[vmem()] * 9,
        out_specs=(vmem(),) * 4,
        scratch_shapes=[
            pltpu.VMEM(big, F32),
            pltpu.VMEM(big, F32),
            pltpu.VMEM(big, F32),
            pltpu.VMEM((LANES, CH), F32),
            pltpu.VMEM((CH, LANES), F32),
            pltpu.VMEM((ROWS, 1, LANES), F32),
            pltpu.VMEM((CH, LANES), F32),
            pltpu.VMEM((HID, LANES), F32),
            pltpu.VMEM((HID, CH), BF16),
            pltpu.VMEM((HID, CH), BF16),
            pltpu.VMEM((CH + 16, 2 * LANES), BF16),
            pltpu.VMEM((CH + 16, HID), F32),
            pltpu.VMEM((HID, CH), F32),
            pltpu.VMEM((CH, LANES), F32),
            pltpu.VMEM((48, 256), F32),
        ],
        compiler_params=pltpu.CompilerParams(vmem_limit_bytes=VMEM_BYTES),
    )(x, cot, land_sea, edges, kernel, gain_row, weight_in, bias_row, w_out_t)

    total_cells = ROWS * LANES * lax.axis_size("dp") * lax.axis_size("lon")
    piece = (4, CH)
    grad_fields, g_in, g_out, g_gain, g_bias, g_kern = pl.pallas_call(
        functools.partial(grad_kernel, scale=1.0 / math.sqrt(total_cells)),
        name="grads",
        out_shape=(
            jax.ShapeDtypeStruct(big, BF16),
            jax.ShapeDtypeStruct((12, HID), F32),
            jax.ShapeDtypeStruct((48, CH), F32),
            jax.ShapeDtypeStruct((1, CH), F32),
            jax.ShapeDtypeStruct((1, HID), F32),
            jax.ShapeDtypeStruct((7, 7, CH), F32),
        ),
        in_specs=[vmem()] * 8,
        out_specs=(vmem(),) * 6,
        scratch_shapes=[
            pltpu.VMEM(big, F32),
            pltpu.VMEM(big, F32),
            pltpu.VMEM(big, F32),
            pltpu.VMEM(big, F32),
            pltpu.VMEM(big, F32),
            pltpu.VMEM((LANES, CH), F32),
            pltpu.VMEM((CH, LANES), F32),
            pltpu.VMEM((CH, LANES), F32),
            pltpu.VMEM((4 * PEERS, CH), F32),
            pltpu.VMEM((2, CH, LANES), BF16),
            pltpu.VMEM((PEERS, 48, 256), BF16),
            pltpu.VMEM((PEERS, 48, 256), BF16),
            pltpu.VMEM((PEERS, 48, 256), BF16),
            pltpu.VMEM((48, 256), BF16),
            pltpu.VMEM((PEERS // 2, 48, 256), BF16),
            pltpu.VMEM((48, 256), F32),
            pltpu.VMEM((48, 256), F32),
            pltpu.VMEM((PEERS,) + piece, F32),
            pltpu.VMEM((PEERS,) + piece, F32),
            pltpu.VMEM(piece, F32),
            pltpu.VMEM((PEERS,) + piece, F32),
            pltpu.VMEM(piece, F32),
            pltpu.VMEM((PEERS,) + piece, F32),
            dma((2,)),
            dma((2,)),
            dma((2,)),
            dma((2,)),
            dma((PEERS,)),
            dma((PEERS,)),
            dma((PEERS // 2,)),
            dma((PEERS // 2,)),
            dma((PEERS,)),
            dma((PEERS,)),
            dma((PEERS,)),
            dma((PEERS,)),
            dma((PEERS,)),
            dma((PEERS,)),
        ],
        compiler_params=pltpu.CompilerParams(
            collective_id=1, has_side_effects=True, vmem_limit_bytes=VMEM_BYTES
        ),
    )(x, cot, land_sea, edges, kernel, d_conv, d_edges, parts)

    def back(y):
        return jnp.transpose(y[None], (0, 1, 3, 2))

    return (
        back(out),
        back(grad_fields),
        g_in,
        g_out,
        g_kern,
        g_gain.reshape(CH),
        g_bias.reshape(HID),
    )


def solution(mesh):
    placed = (
        P("dp", None, "lon", None),
        P("dp", None, "lon", None),
        P(None, "lon"),
        P(),
        P(),
        P(),
        P(),
        P(),
    )
    return jax.shard_map(
        per_device,
        mesh=mesh,
        in_specs=placed,
        out_specs=(
            P("dp", None, "lon", None),
            P("dp", None, "lon", None),
            P("dp", None),
            P("dp", None),
            P(),
            P(),
            P(),
        ),
        check_vma=False,
    )
```

```python
import functools
import math

import jax
import jax.numpy as jnp
from jax import lax
from jax.experimental import pallas as pl
from jax.experimental.pallas import tpu as pltpu
from jax.sharding import PartitionSpec as P

F32 = jnp.float32
BF16 = jnp.bfloat16
MESH = pl.DeviceIdType.MESH
ROWS = 16
CH = 192
HID = 768
LANES = 128
TILES = CH // 8
PEERS = 16
VMEM_BYTES = 60 * 1024 * 1024


def lane_ids(shape):
    return lax.broadcasted_iota(jnp.int32, shape, 1)


def pack_edges(row_of):
    group = ((lane_ids((CH, LANES)) + 4) // 8) % ROWS
    packed = jnp.zeros((CH, LANES), F32)
    for i in range(ROWS):
        row = row_of(i)
        if i:
            row = pltpu.roll(row, 8 * i, axis=1)
        packed = jnp.where(group == i, row, packed)
    return packed


def merge_edges(from_left, from_right):
    low = lane_ids((CH, LANES)) % 8 < 4
    return jnp.where(low, from_right.astype(F32), from_left.astype(F32))


def spread_edges(edges, halo_ref):
    for i in range(ROWS):
        halo_ref[i] = pltpu.roll(edges, (LANES - 8 * i) % LANES, axis=1) if i else edges


def shifted_rows(src, halo, c0, shift):
    lane = lane_ids((8, LANES))
    rows = []
    for r in range(ROWS):
        row = src[r, pl.ds(c0, 8), :]
        if shift > 0:
            row = jnp.where(lane < shift, halo[r, pl.ds(c0, 8), :], row)
        elif shift < 0:
            row = jnp.where(lane >= LANES + shift, halo[r, pl.ds(c0, 8), :], row)
        if shift:
            row = pltpu.roll(row, (LANES - shift) % LANES, axis=1)
        rows.append(row)
    return rows


def conv_tile(src, halo, taps, dst, tile, sign):
    c0 = pl.multiple_of(tile * 8, 8)
    weights = taps[pl.ds(c0, 8), :]
    total = [None] * ROWS
    for b in range(7):
        rows = shifted_rows(src, halo, c0, sign * (b - 3))
        for a in range(7):
            col = 8 * a + b
            w = jnp.broadcast_to(weights[:, col : col + 1], (8, LANES))
            for i in range(ROWS):
                r = i + sign * (a - 3)
                if 0 <= r < ROWS:
                    term = w * rows[r]
                    total[i] = term if total[i] is None else total[i] + term
    for i in range(ROWS):
        dst[i // 2, pl.ds(c0, 8), LANES * (i % 2) : LANES * (i % 2) + LANES] = total[i]


def kernel_grad_tile(src, halo, grad, dst, tile):
    c0 = pl.multiple_of(tile * 8, 8)
    lane = lane_ids((8, LANES))
    out = jnp.zeros((8, LANES), F32)
    for b in range(7):
        rows = shifted_rows(src, halo, c0, b - 3)
        sums = [None] * 7
        for i in range(ROWS):
            g = grad[i, pl.ds(c0, 8), :]
            for a in range(7):
                r = i + a - 3
                if 0 <= r < ROWS:
                    term = g * rows[r]
                    sums[a] = term if sums[a] is None else sums[a] + term
        for a in range(7):
            col = jnp.sum(sums[a], axis=1, keepdims=True)
            out = jnp.where(lane == 8 * a + b, col, out)
    dst[pl.ds(c0, 8), :] = out


def load_taps(kern_ref, stage, taps):
    stage[...] = jnp.zeros_like(stage)
    for a in range(7):
        stage[8 * a : 8 * a + 7, :] = kern_ref[a]
    taps[...] = jnp.transpose(stage[...])


def ring_neighbours():
    me = lax.axis_index("lon")
    return lax.rem(me + PEERS - 1, PEERS), lax.rem(me + 1, PEERS)


def lon_device(lon):
    return (lax.axis_index("dp"), lon)


def gelu_terms(z):
    half = 0.5 * (1.0 + lax.erf(z * (1.0 / math.sqrt(2.0))))
    slope = half + z * (jnp.exp(z * z * -0.5) * (1.0 / math.sqrt(2.0 * math.pi)))
    return z * half, slope


def loop(lo, hi, step):
    def body(t, carry):
        step(t)
        return carry

    lax.fori_loop(lo, hi, body, 0)


def half(i):
    return slice(LANES * (i % 2), LANES * (i % 2) + LANES)


def main_kernel(
    fields, cot_hbm, mask, kern, gain_row, w_in_hbm, bias_row, w_out_t_hbm,
    out_hbm, grad_fields, totals, kern_total,
    cot, w_in_raw, w_out_t_raw, out,
    masked, m_halo, grad, d_halo, conv, branch, d_normed,
    stage, taps, taps_grad, m3, gain_col, bias_col,
    w_in_t, w_in, w_out, w_out_t, aug, gm, inv,
    part_in, part_out, gain_sum, block,
    m_edges, m_slots, d_edges, d_slots,
    parts, sib_in, half_sum, dp_in, dp_sum, lon_in, total, sib_total,
    k_pieces, k_lon, k_sum, k_dp, k_full, k_all,
    load_sem, m_send, m_recv, d_send, d_recv, sib_send, sib_recv, last_send, last_recv,
    dp_send, dp_recv, lon_send, lon_recv,
    ks_send, ks_recv, kd_send, kd_recv, kg_send, kg_recv,
):
    dp, lon = lax.axis_index("dp"), lax.axis_index("lon")
    left, right = ring_neighbours()
    core = lax.rem(lon, 2)
    sibling = lon + 1 - 2 * core
    barrier = pltpu.get_barrier_semaphore()

    def dp_peer(k):
        return (lax.rem(dp + k, PEERS), lon)

    def lon_peer(k):
        return (dp, lax.rem(lon + k, PEERS))

    def greet(k):
        pl.semaphore_signal(barrier, inc=1, device_id=dp_peer(k), device_id_type=MESH)
        pl.semaphore_signal(barrier, inc=1, device_id=lon_peer(k), device_id_type=MESH)

    def remote(src, dst, send, recv, device):
        return pltpu.make_async_remote_copy(
            src_ref=src, dst_ref=dst, send_sem=send, recv_sem=recv,
            device_id=device, device_id_type=MESH,
        )

    def field_edge(k):
        peer = (left, right)[k]
        return remote(m_edges, m_slots.at[k], m_send.at[k], m_recv.at[k], lon_device(peer))

    def grad_edge(k):
        peer = (left, right)[k]
        return remote(d_edges, d_slots.at[k], d_send.at[k], d_recv.at[k], lon_device(peer))

    def to_sibling(h):
        return remote(
            parts.at[h, 1 - core], sib_in.at[h], sib_send.at[h], sib_recv.at[h],
            lon_device(sibling),
        )

    def over_dp(h):
        def make(k):
            return remote(
                half_sum.at[h, lax.rem(dp + k, PEERS)], dp_in.at[h, k],
                dp_send.at[h, k], dp_recv.at[h, k], dp_peer(k),
            )

        return make

    def over_lon(k):
        return remote(dp_sum, lon_in.at[k], lon_send.at[k], lon_recv.at[k], lon_peer(2 * k))

    def last_sibling():
        return remote(total, sib_total, last_send, last_recv, lon_device(sibling))

    def kernel_scatter(k):
        return remote(
            k_pieces.at[lax.rem(lon + k, PEERS)], k_lon.at[k], ks_send.at[k], ks_recv.at[k],
            lon_peer(k),
        )

    def kernel_over_dp(k):
        return remote(k_sum, k_dp.at[k], kd_send.at[k], kd_recv.at[k], dp_peer(k))

    def kernel_gather(k):
        return remote(k_full, k_all.at[k], kg_send.at[k], kg_recv.at[k], lon_peer(k))

    def start_all(make, count):
        loop(1, count, lambda k: make(k).start())

    def wait_all(make, count):
        loop(1, count, lambda k: make(k).wait())

    def sum_slots(own, slots, count):
        def body(k, acc):
            return acc + slots[k].astype(F32)

        return lax.fori_loop(1, count, body, own.astype(F32))

    loads = [
        pltpu.make_async_copy(src, dst, load_sem.at[n])
        for n, (src, dst) in enumerate(
            ((w_in_hbm, w_in_raw), (w_out_t_hbm, w_out_t_raw), (cot_hbm, cot))
        )
    ]
    for load in loads:
        load.start()
    loop(1, PEERS, greet)

    maskf = mask[...].astype(F32)
    for i in range(ROWS):
        m3[i] = maskf[i : i + 1, :]
        masked[i] = fields[i].astype(F32) * maskf[i : i + 1, :]
    m_edges[...] = pack_edges(lambda i: masked[i]).astype(BF16)
    pl.semaphore_wait(barrier, 2 * (PEERS - 1))
    for k in range(2):
        field_edge(k).start()

    load_taps(kern, stage, taps)
    gain_col[...] = jnp.transpose(jnp.broadcast_to(gain_row[...], (LANES, CH)))
    bias_wide = jnp.transpose(jnp.broadcast_to(bias_row[...], (LANES, HID)))
    loads[0].wait()
    loads[1].wait()
    in_t = jnp.transpose(w_in_raw[...].astype(F32)).astype(BF16)
    out_n = jnp.transpose(w_out_t_raw[...].astype(F32)).astype(BF16)
    for h in range(3):
        for d in range(PEERS):
            to = slice(16 * d, 16 * d + 16)
            at = slice(48 * d + 16 * h, 48 * d + 16 * h + 16)
            w_in_t[h, to, :] = in_t[at, :]
            w_out[h, to, :] = out_n[at, :]
            bias_col[h, to, :] = bias_wide[at, :]
        w_in[h] = jnp.transpose(w_in_t[h].astype(F32)).astype(BF16)
        w_out_t[h] = jnp.transpose(w_out[h].astype(F32)).astype(BF16)
    ones_row = lax.broadcasted_iota(jnp.int32, (16, 2 * LANES), 0) == 0
    for k in range(ROWS // 2):
        aug[k, CH : CH + 16, :] = jnp.where(ones_row, 1.0, 0.0).astype(BF16)
    gain_sum[...] = jnp.zeros_like(gain_sum)
    block[...] = jnp.zeros_like(block)

    for k in range(2):
        field_edge(k).wait()
    spread_edges(merge_edges(m_slots[1], m_slots[0]), m_halo)
    loop(0, TILES, lambda t: conv_tile(masked, m_halo, taps, conv, t, 1))
    loads[2].wait()

    def pair(ref, k):
        return jnp.concatenate(
            [ref[2 * k].astype(F32), ref[2 * k + 1].astype(F32)], axis=1
        )

    def gain_pair():
        return jnp.concatenate([gain_col[...], gain_col[...]], axis=1)

    def norm_step(k):
        c = conv[k]
        mu = jnp.sum(c, axis=0, keepdims=True) * (1.0 / CH)
        centered = c - mu
        var = jnp.sum(centered * centered, axis=0, keepdims=True) * (1.0 / CH)
        inv_sigma = lax.rsqrt(var + 1e-6)
        nhat = centered * inv_sigma
        inv[k] = inv_sigma
        conv[k] = nhat
        aug[k, 0:CH, :] = (nhat * gain_pair()).astype(BF16)
        gm[k] = (pair(cot, k) * pair(m3, k)).astype(BF16)

    loop(0, ROWS // 2, norm_step)

    def mlp_step(h, k):
        bias2 = jnp.concatenate([bias_col[h], bias_col[h]], axis=1)
        pre = jnp.dot(w_in_t[h], aug[k, 0:CH, :], preferred_element_type=F32) + bias2
        d_act = jnp.dot(w_out[h], gm[k], preferred_element_type=F32)
        act, slope = gelu_terms(pre)
        act = act.astype(BF16)
        d_pre = (d_act * slope).astype(BF16)
        more_branch = jnp.dot(w_out_t[h], act, preferred_element_type=F32)
        more_d = jnp.dot(w_in[h], d_pre, preferred_element_type=F32)
        if h == 0:
            branch[k] = more_branch
            d_normed[k] = more_d
        else:
            branch[k] += more_branch
            d_normed[k] += more_d
        part_in[...] += lax.dot_general(
            aug[k], d_pre, (((1,), (1,)), ((), ())), preferred_element_type=F32
        )
        part_out[...] += lax.dot_general(
            act, gm[k], (((1,), (1,)), ((), ())), preferred_element_type=F32
        )

    def exchange_half(h):
        to_sibling(h).wait()

        def add(d):
            mine = parts[h, core, d].astype(F32)
            half_sum[h, d] = (mine + sib_in[h, d].astype(F32)).astype(BF16)

        loop(0, PEERS, add)
        start_all(over_dp(h), PEERS)

    for h in range(3):
        part_in[...] = jnp.zeros_like(part_in)
        part_out[...] = jnp.zeros_like(part_out)
        loop(0, 4, functools.partial(mlp_step, h))
        if h:
            exchange_half(h - 1)
        loop(4, 8, functools.partial(mlp_step, h))
        for d in range(PEERS):
            block[0:12, :] = part_in[12 * d : 12 * d + 12, :]
            block[12:13, :] = part_in[CH : CH + 1, :]
            parts[h, 0, d] = block[...].astype(BF16)
            parts[h, 1, d, :, 0:CH] = part_out[16 * d : 16 * d + 16, :].astype(BF16)
            parts[h, 1, d, :, CH:256] = jnp.zeros((16, 64), BF16)
        to_sibling(h).start()

    def norm_back(k):
        nhat = conv[k]
        d_n = d_normed[k]
        m2 = pair(m3, k)
        result = (m2 * (pair(fields, k) + branch[k])).astype(BF16)
        along = d_n * nhat
        gain_sum[...] += along[:, :LANES] + along[:, LANES:]
        d_hat = d_n * gain_pair()
        mean_d = jnp.sum(d_hat, axis=0, keepdims=True) * (1.0 / CH)
        mean_dn = jnp.sum(d_hat * nhat, axis=0, keepdims=True) * (1.0 / CH)
        d = inv[k] * (d_hat - mean_d - nhat * mean_dn)
        for j in range(2):
            out[2 * k + j] = result[:, half(j)]
            grad[2 * k + j] = d[:, half(j)]

    loop(0, ROWS // 2, norm_back)
    store = pltpu.make_async_copy(out, out_hbm, load_sem.at[3])
    store.start()
    exchange_half(2)
    d_edges[...] = pack_edges(lambda i: grad[i]).astype(BF16)
    for k in range(2):
        grad_edge(k).start()

    loop(0, TILES, lambda t: kernel_grad_tile(masked, m_halo, grad, taps_grad, t))
    flipped = jnp.transpose(taps_grad[...])
    gain_total = jnp.sum(jnp.transpose(gain_sum[...]), axis=0, keepdims=True)
    stage[0:64, :] = flipped[0:64, :]
    stage[56:57, :] = gain_total
    for p in range(PEERS):
        k_pieces[p] = stage[4 * p : 4 * p + 4, :]
    start_all(kernel_scatter, PEERS)

    for k in range(2):
        grad_edge(k).wait()
    spread_edges(merge_edges(d_slots[1], d_slots[0]), d_halo)

    def spread_step(t):
        conv_tile(grad, d_halo, taps, branch, t, -1)

    loop(0, 8, spread_step)
    wait_all(kernel_scatter, PEERS)
    k_sum[...] = sum_slots(k_pieces[lon], k_lon, PEERS)
    start_all(kernel_over_dp, PEERS)
    for h in range(3):
        wait_all(over_dp(h), PEERS)
        dp_sum[h] = sum_slots(half_sum[h, dp], dp_in.at[h], PEERS).astype(BF16)
    start_all(over_lon, PEERS // 2)
    loop(8, 16, spread_step)
    wait_all(kernel_over_dp, PEERS)
    k_full[...] = sum_slots(k_sum[...], k_dp, PEERS)
    start_all(kernel_gather, PEERS)
    wait_all(over_lon, PEERS // 2)
    for h in range(3):
        total[h] = sum_slots(dp_sum[h], lon_in.at[:, h], PEERS // 2)
    last_sibling().start()
    loop(16, TILES, spread_step)

    for i in range(ROWS):
        m = maskf[i : i + 1, :]
        grad_fields[i] = (m * (cot[i].astype(F32) + branch[i // 2, :, half(i)])).astype(BF16)

    wait_all(kernel_gather, PEERS)
    k_all[0] = k_full[...]
    for p in range(PEERS):
        kern_total[4 * p : 4 * p + 4, :] = k_all[lax.rem(lon - p + PEERS, PEERS)]
    last_sibling().wait()
    mine, other = total[...], sib_total[...]
    even = core == 0
    totals[0] = jnp.where(even, mine, other)
    totals[1] = jnp.where(even, other, mine)
    store.wait()


def finish_kernel(
    out_in, grad_in, totals, kern_total,
    out, grad, g_in, g_out, g_gain, g_bias, g_kern,
    wide, tall, sems, *, scale
):
    copies = []
    for n in range(4):
        rows = pl.ds(4 * n, 4)
        copies.append(pltpu.make_async_copy(out_in.at[rows], out.at[rows], sems.at[n]))
        copies.append(pltpu.make_async_copy(grad_in.at[rows], grad.at[rows], sems.at[4 + n]))
    for copy in copies:
        copy.start()
    for h in range(3):
        turned = jnp.transpose(totals[0, h] * scale)
        for d in range(PEERS):
            tall[48 * d + 16 * h : 48 * d + 16 * h + 16, :] = turned[16 * d : 16 * d + 16, :]
        g_out[16 * h : 16 * h + 16, :] = totals[1, h, :, 0:CH] * scale
    wide[...] = jnp.transpose(tall[...])
    g_in[...] = wide[0:12, :]
    g_bias[...] = wide[12:13, :]
    g_gain[...] = kern_total[56:57, :] * scale
    for a in range(7):
        g_kern[a] = kern_total[8 * a : 8 * a + 7, :] * scale
    for copy in copies:
        copy.wait()


def vmem():
    return pl.BlockSpec(memory_space=pltpu.VMEM)


def anywhere():
    return pl.BlockSpec(memory_space=pl.ANY)


def per_device(fields, cotangent, land_sea, kernel, ln_gain, weight_in, bias_in, weight_out):
    x = jnp.transpose(fields, (0, 1, 3, 2)).reshape(ROWS, CH, LANES)
    cot = jnp.transpose(cotangent, (0, 1, 3, 2)).reshape(ROWS, CH, LANES)
    w_out_t = jnp.transpose(weight_out)
    dma = pltpu.SemaphoreType.DMA
    big = (ROWS, CH, LANES)
    pairs = (ROWS // 2, CH, 2 * LANES)
    piece = (4, CH)
    blk = (16, 256)

    out, grad_fields, totals, kern_total = pl.pallas_call(
        main_kernel,
        name="block_and_grads",
        out_shape=(
            jax.ShapeDtypeStruct(big, BF16),
            jax.ShapeDtypeStruct(big, BF16),
            jax.ShapeDtypeStruct((2, 3) + blk, F32),
            jax.ShapeDtypeStruct((64, CH), F32),
        ),
        in_specs=[vmem(), anywhere(), vmem(), vmem(), vmem(), anywhere(), vmem(), anywhere()],
        out_specs=(anywhere(), vmem(), vmem(), vmem()),
        scratch_shapes=[
            pltpu.VMEM(big, BF16),
            pltpu.VMEM((CH, HID), BF16),
            pltpu.VMEM((CH, HID), BF16),
            pltpu.VMEM(big, BF16),
            pltpu.VMEM(big, F32),
            pltpu.VMEM(big, F32),
            pltpu.VMEM(big, F32),
            pltpu.VMEM(big, F32),
            pltpu.VMEM(pairs, F32),
            pltpu.VMEM(pairs, F32),
            pltpu.VMEM(pairs, F32),
            pltpu.VMEM((LANES, CH), F32),
            pltpu.VMEM((CH, LANES), F32),
            pltpu.VMEM((CH, LANES), F32),
            pltpu.VMEM((ROWS, 1, LANES), F32),
            pltpu.VMEM((CH, LANES), F32),
            pltpu.VMEM((3, 256, LANES), F32),
            pltpu.VMEM((3, 256, CH), BF16),
            pltpu.VMEM((3, CH, 256), BF16),
            pltpu.VMEM((3, 256, CH), BF16),
            pltpu.VMEM((3, CH, 256), BF16),
            pltpu.VMEM((ROWS // 2, CH + 16, 2 * LANES), BF16),
            pltpu.VMEM(pairs, BF16),
            pltpu.VMEM((ROWS // 2, 1, 2 * LANES), F32),
            pltpu.VMEM((CH + 16, 256), F32),
            pltpu.VMEM((256, CH), F32),
            pltpu.VMEM((CH, LANES), F32),
            pltpu.VMEM(blk, F32),
            pltpu.VMEM((CH, LANES), BF16),
            pltpu.VMEM((2, CH, LANES), BF16),
            pltpu.VMEM((CH, LANES), BF16),
            pltpu.VMEM((2, CH, LANES), BF16),
            pltpu.VMEM((3, 2, PEERS) + blk, BF16),
            pltpu.VMEM((3, PEERS) + blk, BF16),
            pltpu.VMEM((3, PEERS) + blk, BF16),
            pltpu.VMEM((3, PEERS) + blk, BF16),
            pltpu.VMEM((3,) + blk, BF16),
            pltpu.VMEM((PEERS // 2, 3) + blk, BF16),
            pltpu.VMEM((3,) + blk, F32),
            pltpu.VMEM((3,) + blk, F32),
            pltpu.VMEM((PEERS,) + piece, F32),
            pltpu.VMEM((PEERS,) + piece, F32),
            pltpu.VMEM(piece, F32),
            pltpu.VMEM((PEERS,) + piece, F32),
            pltpu.VMEM(piece, F32),
            pltpu.VMEM((PEERS,) + piece, F32),
            dma((4,)),
            dma((2,)),
            dma((2,)),
            dma((2,)),
            dma((2,)),
            dma((3,)),
            dma((3,)),
            dma,
            dma,
            dma((3, PEERS)),
            dma((3, PEERS)),
            dma((PEERS // 2,)),
            dma((PEERS // 2,)),
            dma((PEERS,)),
            dma((PEERS,)),
            dma((PEERS,)),
            dma((PEERS,)),
            dma((PEERS,)),
            dma((PEERS,)),
        ],
        compiler_params=pltpu.CompilerParams(
            collective_id=0, has_side_effects=True, vmem_limit_bytes=VMEM_BYTES
        ),
    )(x, cot, land_sea, kernel, ln_gain.reshape(1, CH), weight_in, bias_in.reshape(1, HID), w_out_t)

    total_cells = ROWS * LANES * lax.axis_size("dp") * lax.axis_size("lon")
    out, grad_fields, g_in, g_out, g_gain, g_bias, g_kern = pl.pallas_call(
        functools.partial(finish_kernel, scale=1.0 / math.sqrt(total_cells)),
        name="finish",
        out_shape=(
            jax.ShapeDtypeStruct(big, BF16),
            jax.ShapeDtypeStruct(big, BF16),
            jax.ShapeDtypeStruct((12, HID), F32),
            jax.ShapeDtypeStruct((48, CH), F32),
            jax.ShapeDtypeStruct((1, CH), F32),
            jax.ShapeDtypeStruct((1, HID), F32),
            jax.ShapeDtypeStruct((7, 7, CH), F32),
        ),
        in_specs=[anywhere(), anywhere(), vmem(), vmem()],
        out_specs=(anywhere(), anywhere()) + (vmem(),) * 5,
        scratch_shapes=[
            pltpu.VMEM((16, HID), F32),
            pltpu.VMEM((HID, 16), F32),
            dma((8,)),
        ],
    )(out, grad_fields, totals, kern_total)

    def back(y):
        return jnp.transpose(y[None], (0, 1, 3, 2))

    return (
        back(out),
        back(grad_fields),
        g_in,
        g_out,
        g_kern,
        g_gain.reshape(CH),
        g_bias.reshape(HID),
    )


def solution(mesh):
    placed = (
        P("dp", None, "lon", None),
        P("dp", None, "lon", None),
        P(None, "lon"),
        P(),
        P(),
        P(),
        P(),
        P(),
    )
    return jax.shard_map(
        per_device,
        mesh=mesh,
        in_specs=placed,
        out_specs=(
            P("dp", None, "lon", None),
            P("dp", None, "lon", None),
            P("dp", None),
            P("dp", None),
            P(),
            P(),
            P(),
        ),
        check_vma=False,
    )
```

```python
import functools
import math

import jax
import jax.numpy as jnp
from jax import lax
from jax.experimental import pallas as pl
from jax.experimental.pallas import tpu as pltpu
from jax.sharding import PartitionSpec as P

F32 = jnp.float32
BF16 = jnp.bfloat16
MESH = pl.DeviceIdType.MESH
ROWS = 16
CH = 192
HID = 768
LANES = 128
TILES = CH // 16
STEP = 1024
STEPS = ROWS * LANES // STEP
PEERS = 16
VMEM_BYTES = 60 * 1024 * 1024


def lane_ids(shape):
    return lax.broadcasted_iota(jnp.int32, shape, 1)


def pack_edges(row_of):
    group = ((lane_ids((CH, LANES)) + 4) // 8) % ROWS
    packed = jnp.zeros((CH, LANES), BF16)
    for i in range(ROWS):
        row = row_of(i)
        if i:
            row = pltpu.roll(row, 8 * i, axis=1)
        packed = jnp.where(group == i, row, packed)
    return packed


def merge_edges(from_left, from_right):
    return jnp.where(lane_ids((CH, LANES)) % 8 < 4, from_right, from_left)


def spread_edges(edges, halo_ref):
    for i in range(ROWS):
        halo_ref[i] = pltpu.roll(edges, (LANES - 8 * i) % LANES, axis=1) if i else edges


def shifted_rows(src, halo, c0, shift):
    lane = lane_ids((16, LANES))
    rows = []
    for r in range(ROWS):
        row = src[r, pl.ds(c0, 16), :]
        if shift > 0:
            row = jnp.where(lane < shift, halo[r, pl.ds(c0, 16), :], row)
        elif shift < 0:
            row = jnp.where(lane >= LANES + shift, halo[r, pl.ds(c0, 16), :], row)
        if shift:
            row = pltpu.roll(row, (LANES - shift) % LANES, axis=1)
        rows.append(row)
    return rows


def plus(total, term):
    return term if total is None else total + term


def conv_tile(src, halo, taps, dst, tile, sign):
    c0 = pl.multiple_of(tile * 16, 16)
    weights = taps[pl.ds(c0, 16), :]
    for b in range(7):
        rows = shifted_rows(src, halo, c0, sign * (b - 3))
        part = [None] * ROWS
        for a in range(7):
            col = 8 * a + b
            w = jnp.broadcast_to(weights[:, col : col + 1], (16, LANES)).astype(BF16)
            for i in range(ROWS):
                r = i + sign * (a - 3)
                if 0 <= r < ROWS:
                    part[i] = plus(part[i], w * rows[r])
        for i in range(ROWS):
            if b:
                dst[i, pl.ds(c0, 16), :] += part[i].astype(F32)
            else:
                dst[i, pl.ds(c0, 16), :] = part[i].astype(F32)


def kernel_grad_tile(src, halo, grad, dst, tile):
    c0 = pl.multiple_of(tile * 16, 16)
    for b in range(7):
        rows = shifted_rows(src, halo, c0, b - 3)
        sums = [[None] * 7, [None] * 7]
        for i in range(ROWS):
            g = grad[i, pl.ds(c0, 16), :]
            part = sums[i // 8]
            for a in range(7):
                r = i + a - 3
                if 0 <= r < ROWS:
                    part[a] = plus(part[a], g * rows[r])
        for a in range(7):
            both = sums[0][a].astype(F32) + sums[1][a].astype(F32)
            dst[8 * a + b, pl.ds(c0, 16), :] = both.astype(BF16)


def sum_lanes(src):
    lane = lane_ids((LANES, LANES))
    total = jnp.zeros((CH, LANES), F32)
    for a in range(7):
        for b in range(7):
            pick = jnp.where(lane == 8 * a + b, 1.0, 0.0).astype(BF16)
            total = total + jnp.dot(src[8 * a + b], pick, preferred_element_type=F32)
    return total


def load_taps(kern_ref, stage, taps):
    stage[...] = jnp.zeros_like(stage)
    for a in range(7):
        stage[8 * a : 8 * a + 7, :] = kern_ref[a]
    taps[...] = jnp.transpose(stage[...])


def ring_neighbours():
    me = lax.axis_index("lon")
    return lax.rem(me + PEERS - 1, PEERS), lax.rem(me + 1, PEERS)


def lon_device(lon):
    return (lax.axis_index("dp"), lon)


def gelu_terms(z):
    half = 0.5 * (1.0 + lax.erf(z * (1.0 / math.sqrt(2.0))))
    slope = half + z * (jnp.exp(z * z * -0.5) * (1.0 / math.sqrt(2.0 * math.pi)))
    return z * half, slope


def loop(lo, hi, step):
    def body(t, carry):
        step(t)
        return carry

    lax.fori_loop(lo, hi, body, 0)


def main_kernel(
    fields, cot_hbm, mask, kern, gain_row, w_in_hbm, bias_row, w_out_t_hbm,
    out_hbm, grad_fields, totals, kern_total,
    cot, w_in_raw, w_out_t_raw, out,
    masked, m_halo, grad, d_halo, conv, branch, d_normed,
    stage, taps, tap_sums, m3, gain_col, bias_col,
    w_in_t, w_in, w_out, w_out_t, aug, gm, inv,
    part_in, part_out, gain_sum, block,
    m_edges, m_slots, d_edges, d_slots,
    parts, sib_in, half_sum, dp_in, dp_sum, lon_in, total, sib_total,
    k_pieces, k_lon, k_sum, k_dp, k_full, k_all,
    load_sem, m_send, m_recv, d_send, d_recv, sib_send, sib_recv, last_send, last_recv,
    dp_send, dp_recv, lon_send, lon_recv,
    ks_send, ks_recv, kd_send, kd_recv, kg_send, kg_recv,
):
    dp, lon = lax.axis_index("dp"), lax.axis_index("lon")
    left, right = ring_neighbours()
    core = lax.rem(lon, 2)
    sibling = lon + 1 - 2 * core
    barrier = pltpu.get_barrier_semaphore()

    def dp_peer(k):
        return (lax.rem(dp + k, PEERS), lon)

    def lon_peer(k):
        return (dp, lax.rem(lon + k, PEERS))

    def greet(k):
        pl.semaphore_signal(barrier, inc=1, device_id=dp_peer(k), device_id_type=MESH)
        pl.semaphore_signal(barrier, inc=1, device_id=lon_peer(k), device_id_type=MESH)

    def remote(src, dst, send, recv, device):
        return pltpu.make_async_remote_copy(
            src_ref=src, dst_ref=dst, send_sem=send, recv_sem=recv,
            device_id=device, device_id_type=MESH,
        )

    def field_edge(k):
        peer = (left, right)[k]
        return remote(m_edges, m_slots.at[k], m_send.at[k], m_recv.at[k], lon_device(peer))

    def grad_edge(k):
        peer = (left, right)[k]
        return remote(d_edges, d_slots.at[k], d_send.at[k], d_recv.at[k], lon_device(peer))

    def to_sibling(h):
        return remote(
            parts.at[h, 1 - core], sib_in.at[h], sib_send.at[h], sib_recv.at[h],
            lon_device(sibling),
        )

    def over_dp(h):
        def make(k):
            return remote(
                half_sum.at[h, lax.rem(dp + k, PEERS)], dp_in.at[h, k],
                dp_send.at[h, k], dp_recv.at[h, k], dp_peer(k),
            )

        return make

    def over_lon(k):
        return remote(dp_sum, lon_in.at[k], lon_send.at[k], lon_recv.at[k], lon_peer(2 * k))

    def last_sibling():
        return remote(total, sib_total, last_send, last_recv, lon_device(sibling))

    def kernel_scatter(k):
        return remote(
            k_pieces.at[lax.rem(lon + k, PEERS)], k_lon.at[k], ks_send.at[k], ks_recv.at[k],
            lon_peer(k),
        )

    def kernel_over_dp(k):
        return remote(k_sum, k_dp.at[k], kd_send.at[k], kd_recv.at[k], dp_peer(k))

    def kernel_gather(k):
        return remote(k_full, k_all.at[k], kg_send.at[k], kg_recv.at[k], lon_peer(k))

    def start_all(make, count):
        loop(1, count, lambda k: make(k).start())

    def wait_all(make, count):
        loop(1, count, lambda k: make(k).wait())

    def sum_slots(own, slots, count):
        def body(k, acc):
            return acc + slots[k].astype(F32)

        return lax.fori_loop(1, count, body, own.astype(F32))

    loads = [
        pltpu.make_async_copy(src, dst, load_sem.at[n])
        for n, (src, dst) in enumerate(
            ((w_in_hbm, w_in_raw), (w_out_t_hbm, w_out_t_raw), (cot_hbm, cot))
        )
    ]
    for load in loads:
        load.start()
    loop(1, PEERS, greet)

    maskf = mask[...].astype(F32)
    for i in range(ROWS):
        m3[i] = maskf[i : i + 1, :]
        masked[i] = (fields[i].astype(F32) * maskf[i : i + 1, :]).astype(BF16)
    m_edges[...] = pack_edges(lambda i: masked[i])
    pl.semaphore_wait(barrier, 2 * (PEERS - 1))
    for k in range(2):
        field_edge(k).start()

    load_taps(kern, stage, taps)
    gain_col[...] = jnp.transpose(jnp.broadcast_to(gain_row[...], (LANES, CH)))
    bias_wide = jnp.transpose(jnp.broadcast_to(bias_row[...], (LANES, HID)))
    loads[0].wait()
    loads[1].wait()
    in_t = jnp.transpose(w_in_raw[...].astype(F32)).astype(BF16)
    out_n = jnp.transpose(w_out_t_raw[...].astype(F32)).astype(BF16)
    for h in range(3):
        for d in range(PEERS):
            to = slice(16 * d, 16 * d + 16)
            at = slice(48 * d + 16 * h, 48 * d + 16 * h + 16)
            w_in_t[h, to, :] = in_t[at, :]
            w_out[h, to, :] = out_n[at, :]
            bias_col[h, to, :] = bias_wide[at, :]
        w_in[h] = jnp.transpose(w_in_t[h].astype(F32)).astype(BF16)
        w_out_t[h] = jnp.transpose(w_out[h].astype(F32)).astype(BF16)
    ones_row = lax.broadcasted_iota(jnp.int32, (16, STEP), 0) == 0
    for k in range(STEPS):
        aug[k, CH : CH + 16, :] = jnp.where(ones_row, 1.0, 0.0).astype(BF16)
    gain_sum[...] = jnp.zeros_like(gain_sum)
    block[...] = jnp.zeros_like(block)

    for k in range(2):
        field_edge(k).wait()
    spread_edges(merge_edges(m_slots[1], m_slots[0]), m_halo)
    loop(0, TILES, lambda t: conv_tile(masked, m_halo, taps, conv, t, 1))
    loads[2].wait()

    def place(i):
        per = STEP // LANES
        return i // per, pl.ds(pl.multiple_of((i % per) * LANES, LANES), LANES)

    def norm_step(i):
        k, lanes = place(i)
        c = conv[i]
        mu = jnp.sum(c, axis=0, keepdims=True) * (1.0 / CH)
        centered = c - mu
        var = jnp.sum(centered * centered, axis=0, keepdims=True) * (1.0 / CH)
        inv_sigma = lax.rsqrt(var + 1e-6)
        nhat = centered * inv_sigma
        inv[i] = inv_sigma
        conv[i] = nhat
        aug[k, 0:CH, lanes] = (nhat * gain_col[...]).astype(BF16)
        gm[k, :, lanes] = (cot[i].astype(F32) * m3[i]).astype(BF16)

    loop(0, ROWS, norm_step)

    def mlp_step(h, k):
        bias = jnp.concatenate([bias_col[h]] * (STEP // LANES), axis=1)
        pre = jnp.dot(w_in_t[h], aug[k, 0:CH, :], preferred_element_type=F32) + bias
        d_act = jnp.dot(w_out[h], gm[k], preferred_element_type=F32)
        act, slope = gelu_terms(pre)
        act = act.astype(BF16)
        d_pre = (d_act * slope).astype(BF16)
        more_branch = jnp.dot(w_out_t[h], act, preferred_element_type=F32)
        more_d = jnp.dot(w_in[h], d_pre, preferred_element_type=F32)
        if h == 0:
            branch[k] = more_branch
            d_normed[k] = more_d
        else:
            branch[k] += more_branch
            d_normed[k] += more_d
        more_in = lax.dot_general(
            aug[k], d_pre, (((1,), (1,)), ((), ())), preferred_element_type=F32
        )
        more_out = lax.dot_general(
            act, gm[k], (((1,), (1,)), ((), ())), preferred_element_type=F32
        )
        if k == 0:
            part_in[...] = more_in
            part_out[...] = more_out
        else:
            part_in[...] += more_in
            part_out[...] += more_out

    def exchange_half(h):
        to_sibling(h).wait()

        def add(d):
            mine = parts[h, core, d].astype(F32)
            half_sum[h, d] = (mine + sib_in[h, d].astype(F32)).astype(BF16)

        loop(0, PEERS, add)
        start_all(over_dp(h), PEERS)

    for h in range(3):
        mlp_step(h, 0)
        if h:
            exchange_half(h - 1)
        mlp_step(h, 1)
        for d in range(PEERS):
            block[0:12, :] = part_in[12 * d : 12 * d + 12, :]
            block[12:13, :] = part_in[CH : CH + 1, :]
            parts[h, 0, d] = block[...].astype(BF16)
            parts[h, 1, d, :, 0:CH] = part_out[16 * d : 16 * d + 16, :].astype(BF16)
            parts[h, 1, d, :, CH:256] = jnp.zeros((16, 64), BF16)
        to_sibling(h).start()

    def norm_back(i):
        k, lanes = place(i)
        nhat = conv[i]
        d_n = d_normed[k, :, lanes]
        out[i] = (m3[i] * (fields[i].astype(F32) + branch[k, :, lanes])).astype(BF16)
        gain_sum[...] += d_n * nhat
        d_hat = d_n * gain_col[...]
        mean_d = jnp.sum(d_hat, axis=0, keepdims=True) * (1.0 / CH)
        mean_dn = jnp.sum(d_hat * nhat, axis=0, keepdims=True) * (1.0 / CH)
        grad[i] = (inv[i] * (d_hat - mean_d - nhat * mean_dn)).astype(BF16)

    loop(0, ROWS, norm_back)
    store = pltpu.make_async_copy(out, out_hbm, load_sem.at[3])
    store.start()
    exchange_half(2)
    d_edges[...] = pack_edges(lambda i: grad[i])
    for k in range(2):
        grad_edge(k).start()

    loop(0, TILES, lambda t: kernel_grad_tile(masked, m_halo, grad, tap_sums, t))
    flipped = jnp.transpose(sum_lanes(tap_sums))
    gain_total = jnp.sum(jnp.transpose(gain_sum[...]), axis=0, keepdims=True)
    stage[0:64, :] = flipped[0:64, :]
    stage[56:57, :] = gain_total
    for p in range(PEERS):
        k_pieces[p] = stage[4 * p : 4 * p + 4, :]
    start_all(kernel_scatter, PEERS)

    for k in range(2):
        grad_edge(k).wait()
    spread_edges(merge_edges(d_slots[1], d_slots[0]), d_halo)

    def spread_step(t):
        conv_tile(grad, d_halo, taps, conv, t, -1)

    loop(0, 4, spread_step)
    wait_all(kernel_scatter, PEERS)
    k_sum[...] = sum_slots(k_pieces[lon], k_lon, PEERS)
    start_all(kernel_over_dp, PEERS)
    for h in range(3):
        wait_all(over_dp(h), PEERS)
        dp_sum[h] = sum_slots(half_sum[h, dp], dp_in.at[h], PEERS).astype(BF16)
    start_all(over_lon, PEERS // 2)
    loop(4, 8, spread_step)
    wait_all(kernel_over_dp, PEERS)
    k_full[...] = sum_slots(k_sum[...], k_dp, PEERS)
    start_all(kernel_gather, PEERS)
    wait_all(over_lon, PEERS // 2)
    for h in range(3):
        total[h] = sum_slots(dp_sum[h], lon_in.at[:, h], PEERS // 2)
    last_sibling().start()
    loop(8, TILES, spread_step)

    for i in range(ROWS):
        m = maskf[i : i + 1, :]
        grad_fields[i] = (m * (cot[i].astype(F32) + conv[i])).astype(BF16)

    wait_all(kernel_gather, PEERS)
    k_all[0] = k_full[...]
    for p in range(PEERS):
        kern_total[4 * p : 4 * p + 4, :] = k_all[lax.rem(lon - p + PEERS, PEERS)]
    last_sibling().wait()
    mine, other = total[...], sib_total[...]
    even = core == 0
    totals[0] = jnp.where(even, mine, other)
    totals[1] = jnp.where(even, other, mine)
    store.wait()


def finish_kernel(
    out_in, grad_in, totals, kern_total,
    out, grad, g_in, g_out, g_gain, g_bias, g_kern,
    held, wide, tall, sems, *, scale
):
    steps = []
    for n in range(8):
        rows = pl.ds(4 * (n % 4), 4)
        src, dst = (out_in, out) if n < 4 else (grad_in, grad)
        steps.append(
            (
                pltpu.make_async_copy(src.at[rows], held.at[n], sems.at[0, n]),
                pltpu.make_async_copy(held.at[n], dst.at[rows], sems.at[1, n]),
            )
        )
    for load, _ in steps:
        load.start()
    for load, save in steps:
        load.wait()
        save.start()
    for h in range(3):
        turned = jnp.transpose(totals[0, h] * scale)
        for d in range(PEERS):
            tall[48 * d + 16 * h : 48 * d + 16 * h + 16, :] = turned[16 * d : 16 * d + 16, :]
        g_out[16 * h : 16 * h + 16, :] = totals[1, h, :, 0:CH] * scale
    wide[...] = jnp.transpose(tall[...])
    g_in[...] = wide[0:12, :]
    g_bias[...] = wide[12:13, :]
    g_gain[...] = kern_total[56:57, :] * scale
    for a in range(7):
        g_kern[a] = kern_total[8 * a : 8 * a + 7, :] * scale
    for _, save in steps:
        save.wait()


def vmem():
    return pl.BlockSpec(memory_space=pltpu.VMEM)


def anywhere():
    return pl.BlockSpec(memory_space=pl.ANY)


def per_device(fields, cotangent, land_sea, kernel, ln_gain, weight_in, bias_in, weight_out):
    x = jnp.transpose(fields, (0, 1, 3, 2)).reshape(ROWS, CH, LANES)
    cot = jnp.transpose(cotangent, (0, 1, 3, 2)).reshape(ROWS, CH, LANES)
    w_out_t = jnp.transpose(weight_out)
    dma = pltpu.SemaphoreType.DMA
    big = (ROWS, CH, LANES)
    wide = (STEPS, CH, STEP)
    piece = (4, CH)
    blk = (16, 256)

    out, grad_fields, totals, kern_total = pl.pallas_call(
        main_kernel,
        name="block_and_grads",
        out_shape=(
            jax.ShapeDtypeStruct(big, BF16),
            jax.ShapeDtypeStruct(big, BF16),
            jax.ShapeDtypeStruct((2, 3) + blk, F32),
            jax.ShapeDtypeStruct((64, CH), F32),
        ),
        in_specs=[vmem(), anywhere(), vmem(), vmem(), vmem(), anywhere(), vmem(), anywhere()],
        out_specs=(anywhere(), vmem(), vmem(), vmem()),
        scratch_shapes=[
            pltpu.VMEM(big, BF16),
            pltpu.VMEM((CH, HID), BF16),
            pltpu.VMEM((CH, HID), BF16),
            pltpu.VMEM(big, BF16),
            pltpu.VMEM(big, BF16),
            pltpu.VMEM(big, BF16),
            pltpu.VMEM(big, BF16),
            pltpu.VMEM(big, BF16),
            pltpu.VMEM(big, F32),
            pltpu.VMEM(wide, F32),
            pltpu.VMEM(wide, F32),
            pltpu.VMEM((LANES, CH), F32),
            pltpu.VMEM((CH, LANES), F32),
            pltpu.VMEM((56, CH, LANES), BF16),
            pltpu.VMEM((ROWS, 1, LANES), F32),
            pltpu.VMEM((CH, LANES), F32),
            pltpu.VMEM((3, 256, LANES), F32),
            pltpu.VMEM((3, 256, CH), BF16),
            pltpu.VMEM((3, CH, 256), BF16),
            pltpu.VMEM((3, 256, CH), BF16),
            pltpu.VMEM((3, CH, 256), BF16),
            pltpu.VMEM((STEPS, CH + 16, STEP), BF16),
            pltpu.VMEM(wide, BF16),
            pltpu.VMEM((ROWS, 1, LANES), F32),
            pltpu.VMEM((CH + 16, 256), F32),
            pltpu.VMEM((256, CH), F32),
            pltpu.VMEM((CH, LANES), F32),
            pltpu.VMEM(blk, F32),
            pltpu.VMEM((CH, LANES), BF16),
            pltpu.VMEM((2, CH, LANES), BF16),
            pltpu.VMEM((CH, LANES), BF16),
            pltpu.VMEM((2, CH, LANES), BF16),
            pltpu.VMEM((3, 2, PEERS) + blk, BF16),
            pltpu.VMEM((3, PEERS) + blk, BF16),
            pltpu.VMEM((3, PEERS) + blk, BF16),
            pltpu.VMEM((3, PEERS) + blk, BF16),
            pltpu.VMEM((3,) + blk, BF16),
            pltpu.VMEM((PEERS // 2, 3) + blk, BF16),
            pltpu.VMEM((3,) + blk, F32),
            pltpu.VMEM((3,) + blk, F32),
            pltpu.VMEM((PEERS,) + piece, F32),
            pltpu.VMEM((PEERS,) + piece, F32),
            pltpu.VMEM(piece, F32),
            pltpu.VMEM((PEERS,) + piece, F32),
            pltpu.VMEM(piece, F32),
            pltpu.VMEM((PEERS,) + piece, F32),
            dma((4,)),
            dma((2,)),
            dma((2,)),
            dma((2,)),
            dma((2,)),
            dma((3,)),
            dma((3,)),
            dma,
            dma,
            dma((3, PEERS)),
            dma((3, PEERS)),
            dma((PEERS // 2,)),
            dma((PEERS // 2,)),
            dma((PEERS,)),
            dma((PEERS,)),
            dma((PEERS,)),
            dma((PEERS,)),
            dma((PEERS,)),
            dma((PEERS,)),
        ],
        compiler_params=pltpu.CompilerParams(
            collective_id=0, has_side_effects=True, vmem_limit_bytes=VMEM_BYTES
        ),
    )(x, cot, land_sea, kernel, ln_gain.reshape(1, CH), weight_in, bias_in.reshape(1, HID), w_out_t)

    total_cells = ROWS * LANES * lax.axis_size("dp") * lax.axis_size("lon")
    out, grad_fields, g_in, g_out, g_gain, g_bias, g_kern = pl.pallas_call(
        functools.partial(finish_kernel, scale=1.0 / math.sqrt(total_cells)),
        name="finish",
        out_shape=(
            jax.ShapeDtypeStruct(big, BF16),
            jax.ShapeDtypeStruct(big, BF16),
            jax.ShapeDtypeStruct((12, HID), F32),
            jax.ShapeDtypeStruct((48, CH), F32),
            jax.ShapeDtypeStruct((1, CH), F32),
            jax.ShapeDtypeStruct((1, HID), F32),
            jax.ShapeDtypeStruct((7, 7, CH), F32),
        ),
        in_specs=[anywhere(), anywhere(), vmem(), vmem()],
        out_specs=(anywhere(), anywhere()) + (vmem(),) * 5,
        scratch_shapes=[
            pltpu.VMEM((8, 4, CH, LANES), BF16),
            pltpu.VMEM((16, HID), F32),
            pltpu.VMEM((HID, 16), F32),
            dma((2, 8)),
        ],
    )(out, grad_fields, totals, kern_total)

    def back(y):
        return jnp.transpose(y[None], (0, 1, 3, 2))

    return (
        back(out),
        back(grad_fields),
        g_in,
        g_out,
        g_kern,
        g_gain.reshape(CH),
        g_bias.reshape(HID),
    )


def solution(mesh):
    placed = (
        P("dp", None, "lon", None),
        P("dp", None, "lon", None),
        P(None, "lon"),
        P(),
        P(),
        P(),
        P(),
        P(),
    )
    return jax.shard_map(
        per_device,
        mesh=mesh,
        in_specs=placed,
        out_specs=(
            P("dp", None, "lon", None),
            P("dp", None, "lon", None),
            P("dp", None),
            P("dp", None),
            P(),
            P(),
            P(),
        ),
        check_vma=False,
    )
```

```python
import functools
import math

import jax
import jax.numpy as jnp
from jax import lax
from jax.experimental import pallas as pl
from jax.experimental.pallas import tpu as pltpu
from jax.sharding import PartitionSpec as P

F32 = jnp.float32
BF16 = jnp.bfloat16
MESH = pl.DeviceIdType.MESH
ROWS = 16
CH = 192
HID = 768
LANES = 128
TILES = CH // 16
STEP = 1024
STEPS = ROWS * LANES // STEP
PEERS = 16
VMEM_BYTES = 60 * 1024 * 1024


def lane_ids(shape):
    return lax.broadcasted_iota(jnp.int32, shape, 1)


def pack_edges(row_of):
    group = ((lane_ids((CH, LANES)) + 4) // 8) % ROWS
    packed = jnp.zeros((CH, LANES), BF16)
    for i in range(ROWS):
        row = row_of(i)
        if i:
            row = pltpu.roll(row, 8 * i, axis=1)
        packed = jnp.where(group == i, row, packed)
    return packed


def merge_edges(from_left, from_right):
    return jnp.where(lane_ids((CH, LANES)) % 8 < 4, from_right, from_left)


def spread_edges(edges, halo_ref):
    for i in range(ROWS):
        halo_ref[i] = pltpu.roll(edges, (LANES - 8 * i) % LANES, axis=1) if i else edges


def shifted_rows(src, halo, c0, shift):
    lane = lane_ids((16, LANES))
    rows = []
    for r in range(ROWS):
        row = src[r, pl.ds(c0, 16), :]
        if shift > 0:
            row = jnp.where(lane < shift, halo[r, pl.ds(c0, 16), :], row)
        elif shift < 0:
            row = jnp.where(lane >= LANES + shift, halo[r, pl.ds(c0, 16), :], row)
        if shift:
            row = pltpu.roll(row, (LANES - shift) % LANES, axis=1)
        rows.append(row)
    return rows


def plus(total, term):
    return term if total is None else total + term


def conv_tile(src, halo, taps, dst, tile, sign):
    c0 = pl.multiple_of(tile * 16, 16)
    weights = taps[pl.ds(c0, 16), :]
    for b in range(7):
        rows = shifted_rows(src, halo, c0, sign * (b - 3))
        part = [None] * ROWS
        for a in range(7):
            col = 8 * a + b
            w = jnp.broadcast_to(weights[:, col : col + 1], (16, LANES)).astype(BF16)
            for i in range(ROWS):
                r = i + sign * (a - 3)
                if 0 <= r < ROWS:
                    part[i] = plus(part[i], w * rows[r])
        for i in range(ROWS):
            if b:
                dst[i, pl.ds(c0, 16), :] += part[i].astype(F32)
            else:
                dst[i, pl.ds(c0, 16), :] = part[i].astype(F32)


def kernel_grad_tile(src, halo, grad, dst, tile):
    c0 = pl.multiple_of(tile * 16, 16)
    for b in range(7):
        rows = shifted_rows(src, halo, c0, b - 3)
        sums = [[None] * 7, [None] * 7]
        for i in range(ROWS):
            g = grad[i, pl.ds(c0, 16), :]
            part = sums[i // 8]
            for a in range(7):
                r = i + a - 3
                if 0 <= r < ROWS:
                    part[a] = plus(part[a], g * rows[r])
        for a in range(7):
            both = sums[0][a].astype(F32) + sums[1][a].astype(F32)
            dst[8 * a + b, pl.ds(c0, 16), :] = both.astype(BF16)


def sum_lanes(src):
    lane = lane_ids((LANES, LANES))
    total = jnp.zeros((CH, LANES), F32)
    for a in range(7):
        for b in range(7):
            pick = jnp.where(lane == 8 * a + b, 1.0, 0.0).astype(BF16)
            total = total + jnp.dot(src[8 * a + b], pick, preferred_element_type=F32)
    return total


def load_taps(kern_ref, stage, taps):
    stage[...] = jnp.zeros_like(stage)
    for a in range(7):
        stage[8 * a : 8 * a + 7, :] = kern_ref[a]
    taps[...] = jnp.transpose(stage[...])


def ring_neighbours():
    me = lax.axis_index("lon")
    return lax.rem(me + PEERS - 1, PEERS), lax.rem(me + 1, PEERS)


def lon_device(lon):
    return (lax.axis_index("dp"), lon)


def gelu_terms(z):
    half = 0.5 * (1.0 + lax.erf(z * (1.0 / math.sqrt(2.0))))
    slope = half + z * (jnp.exp(z * z * -0.5) * (1.0 / math.sqrt(2.0 * math.pi)))
    return z * half, slope


def loop(lo, hi, step):
    def body(t, carry):
        step(t)
        return carry

    lax.fori_loop(lo, hi, body, 0)


def main_kernel(
    fields, cot_hbm, mask, kern, gain_row, w_in_hbm, bias_row, w_out_t_hbm,
    out_hbm, grad_fields, totals, kern_total,
    cot, w_in_raw, w_out_t_raw, out,
    masked, m_halo, grad, d_halo, conv, acts, d_normed,
    stage, taps, tap_sums, m3, gain_col, bias_col,
    w_in_t, w_in, w_out, w_out_t, aug, gm, inv,
    part_in, part_out, gain_sum, block,
    m_edges, m_slots, d_edges, d_slots,
    parts, sib_in, half_sum, dp_in, dp_sum, lon_in,
    k_pieces, k_lon, k_sum, k_dp, k_full, k_all,
    load_sem, m_send, m_recv, d_send, d_recv, sib_send, sib_recv,
    dp_send, dp_recv, lon_send, lon_recv,
    ks_send, ks_recv, kd_send, kd_recv, kg_send, kg_recv,
):
    dp, lon = lax.axis_index("dp"), lax.axis_index("lon")
    left, right = ring_neighbours()
    core = lax.rem(lon, 2)
    sibling = lon + 1 - 2 * core
    barrier = pltpu.get_barrier_semaphore()

    def dp_peer(k):
        return (lax.rem(dp + k, PEERS), lon)

    def lon_peer(k):
        return (dp, lax.rem(lon + k, PEERS))

    def greet(k):
        pl.semaphore_signal(barrier, inc=1, device_id=dp_peer(k), device_id_type=MESH)
        pl.semaphore_signal(barrier, inc=1, device_id=lon_peer(k), device_id_type=MESH)

    def remote(src, dst, send, recv, device):
        return pltpu.make_async_remote_copy(
            src_ref=src, dst_ref=dst, send_sem=send, recv_sem=recv,
            device_id=device, device_id_type=MESH,
        )

    def field_edge(k):
        peer = (left, right)[k]
        return remote(m_edges, m_slots.at[k], m_send.at[k], m_recv.at[k], lon_device(peer))

    def grad_edge(k):
        peer = (left, right)[k]
        return remote(d_edges, d_slots.at[k], d_send.at[k], d_recv.at[k], lon_device(peer))

    def to_sibling(h):
        return remote(
            parts.at[h, 1 - core], sib_in.at[h], sib_send.at[h], sib_recv.at[h],
            lon_device(sibling),
        )

    def over_dp(h):
        def make(k):
            return remote(
                half_sum.at[h, lax.rem(dp + k, PEERS)], dp_in.at[h, k],
                dp_send.at[h], dp_recv.at[h], dp_peer(k),
            )

        return make

    def over_lon(h):
        def make(k):
            return remote(
                dp_sum.at[h], lon_in.at[h, k], lon_send.at[h], lon_recv.at[h], lon_peer(k)
            )

        return make

    def kernel_scatter(k):
        return remote(
            k_pieces.at[lax.rem(lon + k, PEERS)], k_lon.at[k], ks_send, ks_recv, lon_peer(k)
        )

    def kernel_over_dp(k):
        return remote(k_sum, k_dp.at[k], kd_send, kd_recv, dp_peer(k))

    def kernel_gather(k):
        return remote(k_full, k_all.at[k], kg_send, kg_recv, lon_peer(k))

    def start_all(make):
        loop(1, PEERS, lambda k: make(k).start())

    def wait_all(slots, sem):
        rows = slots.at[pl.ds(1, PEERS - 1)]
        pltpu.make_async_copy(rows, rows, sem).wait()

    def sum_slots(own, slots, count):
        def body(k, acc):
            return acc + slots[k].astype(F32)

        return lax.fori_loop(1, count, body, own.astype(F32))

    loads = [
        pltpu.make_async_copy(src, dst, load_sem.at[n])
        for n, (src, dst) in enumerate(
            ((w_in_hbm, w_in_raw), (w_out_t_hbm, w_out_t_raw), (cot_hbm, cot))
        )
    ]
    for load in loads:
        load.start()
    loop(1, PEERS, greet)

    maskf = mask[...].astype(F32)
    for i in range(ROWS):
        m3[i] = maskf[i : i + 1, :]
        masked[i] = (fields[i].astype(F32) * maskf[i : i + 1, :]).astype(BF16)
    m_edges[...] = pack_edges(lambda i: masked[i])
    pl.semaphore_wait(barrier, 2 * (PEERS - 1))
    for k in range(2):
        field_edge(k).start()

    load_taps(kern, stage, taps)
    gain_col[...] = jnp.transpose(jnp.broadcast_to(gain_row[...], (LANES, CH)))
    bias_wide = jnp.transpose(jnp.broadcast_to(bias_row[...], (LANES, HID)))
    loads[0].wait()
    loads[1].wait()
    in_t = jnp.transpose(w_in_raw[...].astype(F32)).astype(BF16)
    out_n = jnp.transpose(w_out_t_raw[...].astype(F32)).astype(BF16)
    for h in range(3):
        for d in range(PEERS):
            to = slice(16 * d, 16 * d + 16)
            at = slice(48 * d + 16 * h, 48 * d + 16 * h + 16)
            w_in_t[h, to, :] = in_t[at, :]
            w_out[h, to, :] = out_n[at, :]
            bias_col[h, to, :] = bias_wide[at, :]
        w_in[h] = jnp.transpose(w_in_t[h].astype(F32)).astype(BF16)
        w_out_t[h] = jnp.transpose(w_out[h].astype(F32)).astype(BF16)
    ones_row = lax.broadcasted_iota(jnp.int32, (16, STEP), 0) == 0
    for k in range(STEPS):
        aug[k, CH : CH + 16, :] = jnp.where(ones_row, 1.0, 0.0).astype(BF16)
    gain_sum[...] = jnp.zeros_like(gain_sum)
    block[...] = jnp.zeros_like(block)

    for k in range(2):
        field_edge(k).wait_recv()
    spread_edges(merge_edges(m_slots[1], m_slots[0]), m_halo)
    loop(0, TILES, lambda t: conv_tile(masked, m_halo, taps, conv, t, 1))
    loads[2].wait()

    def place(i):
        per = STEP // LANES
        return i // per, pl.ds(pl.multiple_of((i % per) * LANES, LANES), LANES)

    def norm_step(i):
        k, lanes = place(i)
        c = conv[i]
        mu = jnp.sum(c, axis=0, keepdims=True) * (1.0 / CH)
        centered = c - mu
        var = jnp.sum(centered * centered, axis=0, keepdims=True) * (1.0 / CH)
        inv_sigma = lax.rsqrt(var + 1e-6)
        nhat = centered * inv_sigma
        inv[i] = inv_sigma
        conv[i] = nhat
        aug[k, 0:CH, lanes] = (nhat * gain_col[...]).astype(BF16)
        gm[k, :, lanes] = (cot[i].astype(F32) * m3[i]).astype(BF16)

    loop(0, ROWS, norm_step)

    def mlp_step(h, k):
        bias = jnp.concatenate([bias_col[h]] * (STEP // LANES), axis=1)
        pre = jnp.dot(w_in_t[h], aug[k, 0:CH, :], preferred_element_type=F32) + bias
        d_act = jnp.dot(w_out[h], gm[k], preferred_element_type=F32)
        act, slope = gelu_terms(pre)
        act = act.astype(BF16)
        d_pre = (d_act * slope).astype(BF16)
        acts[h, k] = act
        more_d = jnp.dot(w_in[h], d_pre, preferred_element_type=F32)
        if h == 0:
            d_normed[k] = more_d
        else:
            d_normed[k] += more_d
        more_in = lax.dot_general(
            aug[k], d_pre, (((1,), (1,)), ((), ())), preferred_element_type=F32
        )
        more_out = lax.dot_general(
            act, gm[k], (((1,), (1,)), ((), ())), preferred_element_type=F32
        )
        if k == 0:
            part_in[...] = more_in
            part_out[...] = more_out
        else:
            part_in[...] += more_in
            part_out[...] += more_out

    def exchange_half(h):
        to_sibling(h).wait_recv()

        def add(d):
            mine = parts[h, core, d].astype(F32)
            half_sum[h, d] = (mine + sib_in[h, d].astype(F32)).astype(BF16)

        loop(0, PEERS, add)
        start_all(over_dp(h))

    def exchange_sum(h):
        wait_all(dp_in.at[h], dp_recv.at[h])
        dp_sum[h] = sum_slots(half_sum[h, dp], dp_in.at[h], PEERS).astype(BF16)
        start_all(over_lon(h))

    for h in range(3):
        mlp_step(h, 0)
        if h:
            exchange_half(h - 1)
        mlp_step(h, 1)
        for d in range(PEERS):
            block[0:12, :] = part_in[12 * d : 12 * d + 12, :]
            block[12:13, :] = part_in[CH : CH + 1, :]
            parts[h, 0, d] = block[...].astype(BF16)
            parts[h, 1, d, :, 0:CH] = part_out[16 * d : 16 * d + 16, :].astype(BF16)
            parts[h, 1, d, :, CH:256] = jnp.zeros((16, 64), BF16)
        to_sibling(h).start()

    def norm_back(i):
        k, lanes = place(i)
        nhat = conv[i]
        d_n = d_normed[k, :, lanes]
        gain_sum[...] += d_n * nhat
        d_hat = d_n * gain_col[...]
        mean_d = jnp.sum(d_hat, axis=0, keepdims=True) * (1.0 / CH)
        mean_dn = jnp.sum(d_hat * nhat, axis=0, keepdims=True) * (1.0 / CH)
        grad[i] = (inv[i] * (d_hat - mean_d - nhat * mean_dn)).astype(BF16)

    loop(0, ROWS, norm_back)
    exchange_half(2)
    d_edges[...] = pack_edges(lambda i: grad[i])
    for k in range(2):
        grad_edge(k).start()

    def kernel_step(t):
        kernel_grad_tile(masked, m_halo, grad, tap_sums, t)

    def spread_step(t):
        conv_tile(grad, d_halo, taps, conv, t, -1)

    def branch_step(k):
        branch = jnp.zeros((CH, STEP), F32)
        for h in range(3):
            branch = branch + jnp.dot(w_out_t[h], acts[h, k], preferred_element_type=F32)
        per = STEP // LANES
        for j in range(per):
            i = per * k + j
            kept = fields[i].astype(F32) + branch[:, LANES * j : LANES * j + LANES]
            out[i] = (m3[i] * kept).astype(BF16)

    loop(0, TILES, kernel_step)
    flipped = jnp.transpose(sum_lanes(tap_sums))
    gain_total = jnp.sum(jnp.transpose(gain_sum[...]), axis=0, keepdims=True)
    stage[0:64, :] = flipped[0:64, :]
    stage[56:57, :] = gain_total
    for p in range(PEERS):
        k_pieces[p] = stage[4 * p : 4 * p + 4, :]
    start_all(kernel_scatter)

    exchange_sum(0)
    branch_step(0)
    exchange_sum(1)
    branch_step(1)
    store = pltpu.make_async_copy(out, out_hbm, load_sem.at[3])
    store.start()
    for k in range(2):
        grad_edge(k).wait_recv()
    spread_edges(merge_edges(d_slots[1], d_slots[0]), d_halo)
    wait_all(k_lon, ks_recv)
    k_sum[...] = sum_slots(k_pieces[lon], k_lon, PEERS)
    start_all(kernel_over_dp)
    loop(0, 4, spread_step)
    exchange_sum(2)
    loop(4, TILES, spread_step)
    wait_all(k_dp, kd_recv)
    k_full[...] = sum_slots(k_sum[...], k_dp, PEERS)
    start_all(kernel_gather)

    for i in range(ROWS):
        m = maskf[i : i + 1, :]
        grad_fields[i] = (m * (cot[i].astype(F32) + conv[i])).astype(BF16)

    even = core == 0
    for h in range(3):
        wait_all(lon_in.at[h], lon_recv.at[h])
        mine = dp_sum[h].astype(F32)
        other = lon_in[h, 1].astype(F32)
        for k in range(2, PEERS, 2):
            mine = mine + lon_in[h, k].astype(F32)
            other = other + lon_in[h, k + 1].astype(F32)
        totals[0, h] = jnp.where(even, mine, other)
        totals[1, h] = jnp.where(even, other, mine)
    wait_all(k_all, kg_recv)
    k_all[0] = k_full[...]
    for p in range(PEERS):
        kern_total[4 * p : 4 * p + 4, :] = k_all[lax.rem(lon - p + PEERS, PEERS)]
    for k in range(2):
        field_edge(k).wait_send()
        grad_edge(k).wait_send()
    for h in range(3):
        to_sibling(h).wait_send()
        wait_all(dp_in.at[h], dp_send.at[h])
        wait_all(lon_in.at[h], lon_send.at[h])
    wait_all(k_lon, ks_send)
    wait_all(k_dp, kd_send)
    wait_all(k_all, kg_send)
    store.wait()


def finish_kernel(
    out_in, grad_in, totals, kern_total,
    out, grad, g_in, g_out, g_gain, g_bias, g_kern,
    held, wide, tall, sems, *, scale
):
    steps = []
    for n in range(8):
        rows = pl.ds(4 * (n % 4), 4)
        src, dst = (out_in, out) if n < 4 else (grad_in, grad)
        steps.append(
            (
                pltpu.make_async_copy(src.at[rows], held.at[n], sems.at[0, n]),
                pltpu.make_async_copy(held.at[n], dst.at[rows], sems.at[1, n]),
            )
        )
    for load, _ in steps:
        load.start()
    for load, save in steps:
        load.wait()
        save.start()
    for h in range(3):
        turned = jnp.transpose(totals[0, h] * scale)
        for d in range(PEERS):
            tall[48 * d + 16 * h : 48 * d + 16 * h + 16, :] = turned[16 * d : 16 * d + 16, :]
        g_out[16 * h : 16 * h + 16, :] = totals[1, h, :, 0:CH] * scale
    wide[...] = jnp.transpose(tall[...])
    g_in[...] = wide[0:12, :]
    g_bias[...] = wide[12:13, :]
    g_gain[...] = kern_total[56:57, :] * scale
    for a in range(7):
        g_kern[a] = kern_total[8 * a : 8 * a + 7, :] * scale
    for _, save in steps:
        save.wait()


def vmem():
    return pl.BlockSpec(memory_space=pltpu.VMEM)


def anywhere():
    return pl.BlockSpec(memory_space=pl.ANY)


def per_device(fields, cotangent, land_sea, kernel, ln_gain, weight_in, bias_in, weight_out):
    x = jnp.transpose(fields, (0, 1, 3, 2)).reshape(ROWS, CH, LANES)
    cot = jnp.transpose(cotangent, (0, 1, 3, 2)).reshape(ROWS, CH, LANES)
    w_out_t = jnp.transpose(weight_out)
    dma = pltpu.SemaphoreType.DMA
    big = (ROWS, CH, LANES)
    wide = (STEPS, CH, STEP)
    piece = (4, CH)
    blk = (16, 256)

    out, grad_fields, totals, kern_total = pl.pallas_call(
        main_kernel,
        name="block_and_grads",
        out_shape=(
            jax.ShapeDtypeStruct(big, BF16),
            jax.ShapeDtypeStruct(big, BF16),
            jax.ShapeDtypeStruct((2, 3) + blk, F32),
            jax.ShapeDtypeStruct((64, CH), F32),
        ),
        in_specs=[vmem(), anywhere(), vmem(), vmem(), vmem(), anywhere(), vmem(), anywhere()],
        out_specs=(anywhere(), vmem(), vmem(), vmem()),
        scratch_shapes=[
            pltpu.VMEM(big, BF16),
            pltpu.VMEM((CH, HID), BF16),
            pltpu.VMEM((CH, HID), BF16),
            pltpu.VMEM(big, BF16),
            pltpu.VMEM(big, BF16),
            pltpu.VMEM(big, BF16),
            pltpu.VMEM(big, BF16),
            pltpu.VMEM(big, BF16),
            pltpu.VMEM(big, F32),
            pltpu.VMEM((3, STEPS, 256, STEP), BF16),
            pltpu.VMEM(wide, F32),
            pltpu.VMEM((LANES, CH), F32),
            pltpu.VMEM((CH, LANES), F32),
            pltpu.VMEM((56, CH, LANES), BF16),
            pltpu.VMEM((ROWS, 1, LANES), F32),
            pltpu.VMEM((CH, LANES), F32),
            pltpu.VMEM((3, 256, LANES), F32),
            pltpu.VMEM((3, 256, CH), BF16),
            pltpu.VMEM((3, CH, 256), BF16),
            pltpu.VMEM((3, 256, CH), BF16),
            pltpu.VMEM((3, CH, 256), BF16),
            pltpu.VMEM((STEPS, CH + 16, STEP), BF16),
            pltpu.VMEM(wide, BF16),
            pltpu.VMEM((ROWS, 1, LANES), F32),
            pltpu.VMEM((CH + 16, 256), F32),
            pltpu.VMEM((256, CH), F32),
            pltpu.VMEM((CH, LANES), F32),
            pltpu.VMEM(blk, F32),
            pltpu.VMEM((CH, LANES), BF16),
            pltpu.VMEM((2, CH, LANES), BF16),
            pltpu.VMEM((CH, LANES), BF16),
            pltpu.VMEM((2, CH, LANES), BF16),
            pltpu.VMEM((3, 2, PEERS) + blk, BF16),
            pltpu.VMEM((3, PEERS) + blk, BF16),
            pltpu.VMEM((3, PEERS) + blk, BF16),
            pltpu.VMEM((3, PEERS) + blk, BF16),
            pltpu.VMEM((3,) + blk, BF16),
            pltpu.VMEM((3, PEERS) + blk, BF16),
            pltpu.VMEM((PEERS,) + piece, F32),
            pltpu.VMEM((PEERS,) + piece, F32),
            pltpu.VMEM(piece, F32),
            pltpu.VMEM((PEERS,) + piece, F32),
            pltpu.VMEM(piece, F32),
            pltpu.VMEM((PEERS,) + piece, F32),
            dma((4,)),
            dma((2,)),
            dma((2,)),
            dma((2,)),
            dma((2,)),
            dma((3,)),
            dma((3,)),
            dma((3,)),
            dma((3,)),
            dma((3,)),
            dma((3,)),
            dma,
            dma,
            dma,
            dma,
            dma,
            dma,
        ],
        compiler_params=pltpu.CompilerParams(
            collective_id=0, has_side_effects=True, vmem_limit_bytes=VMEM_BYTES
        ),
    )(x, cot, land_sea, kernel, ln_gain.reshape(1, CH), weight_in, bias_in.reshape(1, HID), w_out_t)

    total_cells = ROWS * LANES * lax.axis_size("dp") * lax.axis_size("lon")
    out, grad_fields, g_in, g_out, g_gain, g_bias, g_kern = pl.pallas_call(
        functools.partial(finish_kernel, scale=1.0 / math.sqrt(total_cells)),
        name="finish",
        out_shape=(
            jax.ShapeDtypeStruct(big, BF16),
            jax.ShapeDtypeStruct(big, BF16),
            jax.ShapeDtypeStruct((12, HID), F32),
            jax.ShapeDtypeStruct((48, CH), F32),
            jax.ShapeDtypeStruct((1, CH), F32),
            jax.ShapeDtypeStruct((1, HID), F32),
            jax.ShapeDtypeStruct((7, 7, CH), F32),
        ),
        in_specs=[anywhere(), anywhere(), vmem(), vmem()],
        out_specs=(anywhere(), anywhere()) + (vmem(),) * 5,
        scratch_shapes=[
            pltpu.VMEM((8, 4, CH, LANES), BF16),
            pltpu.VMEM((16, HID), F32),
            pltpu.VMEM((HID, 16), F32),
            dma((2, 8)),
        ],
    )(out, grad_fields, totals, kern_total)

    def back(y):
        return jnp.transpose(y[None], (0, 1, 3, 2))

    return (
        back(out),
        back(grad_fields),
        g_in,
        g_out,
        g_kern,
        g_gain.reshape(CH),
        g_bias.reshape(HID),
    )


def solution(mesh):
    placed = (
        P("dp", None, "lon", None),
        P("dp", None, "lon", None),
        P(None, "lon"),
        P(),
        P(),
        P(),
        P(),
        P(),
    )
    return jax.shard_map(
        per_device,
        mesh=mesh,
        in_specs=placed,
        out_specs=(
            P("dp", None, "lon", None),
            P("dp", None, "lon", None),
            P("dp", None),
            P("dp", None),
            P(),
            P(),
            P(),
        ),
        check_vma=False,
    )
```

```python
import functools
import math

import jax
import jax.numpy as jnp
from jax import lax
from jax.experimental import pallas as pl
from jax.experimental.pallas import tpu as pltpu
from jax.sharding import PartitionSpec as P

F32 = jnp.float32
BF16 = jnp.bfloat16
MESH = pl.DeviceIdType.MESH
ROWS = 16
CH = 192
HID = 768
LANES = 128
TILES = CH // 16
STEP = 1024
STEPS = ROWS * LANES // STEP
PEERS = 16
VMEM_BYTES = 60 * 1024 * 1024


def lane_ids(shape):
    return lax.broadcasted_iota(jnp.int32, shape, 1)


def pack_edges(row_of):
    group = ((lane_ids((CH, LANES)) + 4) // 8) % ROWS
    packed = jnp.zeros((CH, LANES), BF16)
    for i in range(ROWS):
        row = row_of(i)
        if i:
            row = pltpu.roll(row, 8 * i, axis=1)
        packed = jnp.where(group == i, row, packed)
    return packed


def merge_edges(from_left, from_right):
    return jnp.where(lane_ids((CH, LANES)) % 8 < 4, from_right, from_left)


def spread_edges(edges, halo_ref):
    for i in range(ROWS):
        halo_ref[i] = pltpu.roll(edges, (LANES - 8 * i) % LANES, axis=1) if i else edges


def shifted_rows(src, halo, c0, shift):
    lane = lane_ids((16, LANES))
    rows = []
    for r in range(ROWS):
        row = src[r, pl.ds(c0, 16), :]
        if shift > 0:
            row = jnp.where(lane < shift, halo[r, pl.ds(c0, 16), :], row)
        elif shift < 0:
            row = jnp.where(lane >= LANES + shift, halo[r, pl.ds(c0, 16), :], row)
        if shift:
            row = pltpu.roll(row, (LANES - shift) % LANES, axis=1)
        rows.append(row)
    return rows


def plus(total, term):
    return term if total is None else total + term


def conv_tile(src, halo, taps, dst, tile, sign):
    c0 = pl.multiple_of(tile * 16, 16)
    weights = taps[pl.ds(c0, 16), :]
    for b in range(7):
        rows = shifted_rows(src, halo, c0, sign * (b - 3))
        part = [None] * ROWS
        for a in range(7):
            col = 8 * a + b
            w = jnp.broadcast_to(weights[:, col : col + 1], (16, LANES)).astype(BF16)
            for i in range(ROWS):
                r = i + sign * (a - 3)
                if 0 <= r < ROWS:
                    part[i] = plus(part[i], w * rows[r])
        for i in range(ROWS):
            if b:
                dst[i, pl.ds(c0, 16), :] += part[i].astype(F32)
            else:
                dst[i, pl.ds(c0, 16), :] = part[i].astype(F32)


def kernel_grad_tile(src, halo, grad, dst, tile):
    c0 = pl.multiple_of(tile * 16, 16)
    for b in range(7):
        rows = shifted_rows(src, halo, c0, b - 3)
        sums = [[None] * 7, [None] * 7]
        for i in range(ROWS):
            g = grad[i, pl.ds(c0, 16), :]
            part = sums[i // 8]
            for a in range(7):
                r = i + a - 3
                if 0 <= r < ROWS:
                    part[a] = plus(part[a], g * rows[r])
        for a in range(7):
            both = sums[0][a].astype(F32) + sums[1][a].astype(F32)
            dst[8 * a + b, pl.ds(c0, 16), :] = both.astype(BF16)


def sum_lanes(src):
    lane = lane_ids((LANES, LANES))
    total = jnp.zeros((CH, LANES), F32)
    for a in range(7):
        for b in range(7):
            pick = jnp.where(lane == 8 * a + b, 1.0, 0.0).astype(BF16)
            total = total + jnp.dot(src[8 * a + b], pick, preferred_element_type=F32)
    return total


def load_taps(kern_ref, stage, taps):
    stage[...] = jnp.zeros_like(stage)
    for a in range(7):
        stage[8 * a : 8 * a + 7, :] = kern_ref[a]
    taps[...] = jnp.transpose(stage[...])


def ring_neighbours():
    me = lax.axis_index("lon")
    return lax.rem(me + PEERS - 1, PEERS), lax.rem(me + 1, PEERS)


def lon_device(lon):
    return (lax.axis_index("dp"), lon)


def gelu_terms(z):
    half = 0.5 * (1.0 + lax.erf(z * (1.0 / math.sqrt(2.0))))
    slope = half + z * (jnp.exp(z * z * -0.5) * (1.0 / math.sqrt(2.0 * math.pi)))
    return z * half, slope


def loop(lo, hi, step):
    def body(t, carry):
        step(t)
        return carry

    lax.fori_loop(lo, hi, body, 0)


def main_kernel(
    fields, cot_hbm, mask, kern, gain_row, w_in_hbm, bias_row, w_out_t_hbm,
    out_hbm, grad_fields, totals, kern_total,
    cot, w_in_raw, w_out_t_raw, out,
    masked, m_halo, grad, d_halo, conv, acts, d_normed,
    stage, taps, tap_sums, m3, gain_col, bias_col,
    w_in_t, w_in, w_out, w_out_t, aug, gm, inv,
    part_in, part_out, gain_sum, block,
    m_edges, m_slots, d_edges, d_slots,
    parts, sib_in, half_sum, dp_in, dp_sum, lon_in,
    k_pieces, k_lon, k_sum, k_dp, k_full, k_all,
    load_sem, m_send, m_recv, d_send, d_recv, sib_send, sib_recv,
    dp_send, dp_recv, lon_send, lon_recv,
    ks_send, ks_recv, kd_send, kd_recv, kg_send, kg_recv,
):
    dp, lon = lax.axis_index("dp"), lax.axis_index("lon")
    left, right = ring_neighbours()
    core = lax.rem(lon, 2)
    sibling = lon + 1 - 2 * core
    barrier = pltpu.get_barrier_semaphore()

    def dp_peer(k):
        return (lax.rem(dp + k, PEERS), lon)

    def lon_peer(k):
        return (dp, lax.rem(lon + k, PEERS))

    def greet(k):
        pl.semaphore_signal(barrier, inc=1, device_id=dp_peer(k), device_id_type=MESH)
        pl.semaphore_signal(barrier, inc=1, device_id=lon_peer(k), device_id_type=MESH)

    def remote(src, dst, send, recv, device):
        return pltpu.make_async_remote_copy(
            src_ref=src, dst_ref=dst, send_sem=send, recv_sem=recv,
            device_id=device, device_id_type=MESH,
        )

    def field_edge(k):
        peer = (left, right)[k]
        return remote(m_edges, m_slots.at[k], m_send.at[k], m_recv.at[k], lon_device(peer))

    def grad_edge(k):
        peer = (left, right)[k]
        return remote(d_edges, d_slots.at[k], d_send.at[k], d_recv.at[k], lon_device(peer))

    def to_sibling(h):
        return remote(
            parts.at[h, 1 - core], sib_in.at[h], sib_send.at[h], sib_recv.at[h],
            lon_device(sibling),
        )

    def over_dp(h):
        def make(k):
            return remote(
                half_sum.at[h, lax.rem(dp + k, PEERS)], dp_in.at[h, k],
                dp_send.at[h], dp_recv.at[h], dp_peer(k),
            )

        return make

    def over_lon(h):
        def make(k):
            return remote(
                dp_sum.at[h], lon_in.at[h, k], lon_send.at[h], lon_recv.at[h], lon_peer(k)
            )

        return make

    def kernel_scatter(k):
        return remote(
            k_pieces.at[lax.rem(lon + k, PEERS)], k_lon.at[k], ks_send, ks_recv, lon_peer(k)
        )

    def kernel_over_dp(k):
        return remote(k_sum, k_dp.at[k], kd_send, kd_recv, dp_peer(k))

    def kernel_gather(k):
        return remote(k_full, k_all.at[k], kg_send, kg_recv, lon_peer(k))

    def start_all(make):
        loop(1, PEERS, lambda k: make(k).start())

    def wait_all(slots, sem):
        rows = slots.at[pl.ds(1, PEERS - 1)]
        pltpu.make_async_copy(rows, rows, sem).wait()

    def sum_slots(own, slots, count):
        def body(k, acc):
            return acc + slots[k].astype(F32)

        return lax.fori_loop(1, count, body, own.astype(F32))

    loads = [
        pltpu.make_async_copy(src, dst, load_sem.at[n])
        for n, (src, dst) in enumerate(
            ((w_in_hbm, w_in_raw), (w_out_t_hbm, w_out_t_raw), (cot_hbm, cot))
        )
    ]
    for load in loads:
        load.start()
    loop(1, PEERS, greet)

    maskf = mask[...].astype(F32)
    for i in range(ROWS):
        m3[i] = maskf[i : i + 1, :]
        masked[i] = (fields[i].astype(F32) * maskf[i : i + 1, :]).astype(BF16)
    m_edges[...] = pack_edges(lambda i: masked[i])
    pl.semaphore_wait(barrier, 2 * (PEERS - 1))
    for k in range(2):
        field_edge(k).start()

    load_taps(kern, stage, taps)
    gain_col[...] = jnp.transpose(jnp.broadcast_to(gain_row[...], (LANES, CH)))
    bias_wide = jnp.transpose(jnp.broadcast_to(bias_row[...][None, :], (LANES, HID)))
    loads[0].wait()
    loads[1].wait()
    in_t = jnp.transpose(w_in_raw[...].astype(F32)).astype(BF16)
    out_n = jnp.transpose(w_out_t_raw[...].astype(F32)).astype(BF16)
    for h in range(3):
        for d in range(PEERS):
            to = slice(16 * d, 16 * d + 16)
            at = slice(48 * d + 16 * h, 48 * d + 16 * h + 16)
            w_in_t[h, to, :] = in_t[at, :]
            w_out[h, to, :] = out_n[at, :]
            bias_col[h, to, :] = bias_wide[at, :]
        w_in[h] = jnp.transpose(w_in_t[h].astype(F32)).astype(BF16)
        w_out_t[h] = jnp.transpose(w_out[h].astype(F32)).astype(BF16)
    ones_row = lax.broadcasted_iota(jnp.int32, (16, STEP), 0) == 0
    for k in range(STEPS):
        aug[k, CH : CH + 16, :] = jnp.where(ones_row, 1.0, 0.0).astype(BF16)
    gain_sum[...] = jnp.zeros_like(gain_sum)
    block[...] = jnp.zeros_like(block)

    for k in range(2):
        field_edge(k).wait_recv()
    spread_edges(merge_edges(m_slots[1], m_slots[0]), m_halo)
    loop(0, TILES, lambda t: conv_tile(masked, m_halo, taps, conv, t, 1))
    loads[2].wait()

    def place(i):
        per = STEP // LANES
        return i // per, pl.ds(pl.multiple_of((i % per) * LANES, LANES), LANES)

    def norm_step(i):
        k, lanes = place(i)
        c = conv[i]
        mu = jnp.sum(c, axis=0, keepdims=True) * (1.0 / CH)
        centered = c - mu
        var = jnp.sum(centered * centered, axis=0, keepdims=True) * (1.0 / CH)
        inv_sigma = lax.rsqrt(var + 1e-6)
        nhat = centered * inv_sigma
        inv[i] = inv_sigma
        conv[i] = nhat
        aug[k, 0:CH, lanes] = (nhat * gain_col[...]).astype(BF16)
        gm[k, :, lanes] = (cot[i].astype(F32) * m3[i]).astype(BF16)

    loop(0, ROWS, norm_step)

    def mlp_step(h, k):
        bias = jnp.concatenate([bias_col[h]] * (STEP // LANES), axis=1)
        pre = jnp.dot(w_in_t[h], aug[k, 0:CH, :], preferred_element_type=F32) + bias
        d_act = jnp.dot(w_out[h], gm[k], preferred_element_type=F32)
        act, slope = gelu_terms(pre)
        act = act.astype(BF16)
        d_pre = (d_act * slope).astype(BF16)
        acts[h, k] = act
        more_d = jnp.dot(w_in[h], d_pre, preferred_element_type=F32)
        if h == 0:
            d_normed[k] = more_d
        else:
            d_normed[k] += more_d
        more_in = lax.dot_general(
            aug[k], d_pre, (((1,), (1,)), ((), ())), preferred_element_type=F32
        )
        more_out = lax.dot_general(
            act, gm[k], (((1,), (1,)), ((), ())), preferred_element_type=F32
        )
        if k == 0:
            part_in[...] = more_in
            part_out[...] = more_out
        else:
            part_in[...] += more_in
            part_out[...] += more_out

    def exchange_half(h):
        to_sibling(h).wait_recv()

        def add(d):
            mine = parts[h, core, d].astype(F32)
            half_sum[h, d] = (mine + sib_in[h, d].astype(F32)).astype(BF16)

        loop(0, PEERS, add)
        start_all(over_dp(h))

    def exchange_sum(h):
        wait_all(dp_in.at[h], dp_recv.at[h])
        dp_sum[h] = sum_slots(half_sum[h, dp], dp_in.at[h], PEERS).astype(BF16)
        start_all(over_lon(h))

    for h in range(3):
        mlp_step(h, 0)
        if h:
            exchange_half(h - 1)
        mlp_step(h, 1)
        for d in range(PEERS):
            block[0:12, :] = part_in[12 * d : 12 * d + 12, :]
            block[12:13, :] = part_in[CH : CH + 1, :]
            parts[h, 0, d] = block[...].astype(BF16)
            parts[h, 1, d, :, 0:CH] = part_out[16 * d : 16 * d + 16, :].astype(BF16)
            parts[h, 1, d, :, CH:256] = jnp.zeros((16, 64), BF16)
        to_sibling(h).start()

    def norm_back(i):
        k, lanes = place(i)
        nhat = conv[i]
        d_n = d_normed[k, :, lanes]
        gain_sum[...] += d_n * nhat
        d_hat = d_n * gain_col[...]
        mean_d = jnp.sum(d_hat, axis=0, keepdims=True) * (1.0 / CH)
        mean_dn = jnp.sum(d_hat * nhat, axis=0, keepdims=True) * (1.0 / CH)
        grad[i] = (inv[i] * (d_hat - mean_d - nhat * mean_dn)).astype(BF16)

    loop(0, ROWS, norm_back)
    exchange_half(2)
    d_edges[...] = pack_edges(lambda i: grad[i])
    for k in range(2):
        grad_edge(k).start()

    def kernel_step(t):
        kernel_grad_tile(masked, m_halo, grad, tap_sums, t)

    def spread_step(t):
        conv_tile(grad, d_halo, taps, conv, t, -1)

    def branch_step(k):
        branch = jnp.zeros((CH, STEP), F32)
        for h in range(3):
            branch = branch + jnp.dot(w_out_t[h], acts[h, k], preferred_element_type=F32)
        per = STEP // LANES
        for j in range(per):
            i = per * k + j
            kept = fields[i].astype(F32) + branch[:, LANES * j : LANES * j + LANES]
            out[i] = (m3[i] * kept).astype(BF16)

    loop(0, TILES, kernel_step)
    flipped = jnp.transpose(sum_lanes(tap_sums))
    gain_total = jnp.sum(jnp.transpose(gain_sum[...]), axis=0, keepdims=True)
    stage[0:64, :] = flipped[0:64, :]
    stage[56:57, :] = gain_total
    for p in range(PEERS):
        k_pieces[p] = stage[4 * p : 4 * p + 4, :]
    start_all(kernel_scatter)

    exchange_sum(0)
    branch_step(0)
    exchange_sum(1)
    branch_step(1)
    store = pltpu.make_async_copy(out, out_hbm, load_sem.at[3])
    store.start()
    for k in range(2):
        grad_edge(k).wait_recv()
    spread_edges(merge_edges(d_slots[1], d_slots[0]), d_halo)
    wait_all(k_lon, ks_recv)
    k_sum[...] = sum_slots(k_pieces[lon], k_lon, PEERS)
    start_all(kernel_over_dp)
    loop(0, 4, spread_step)
    exchange_sum(2)
    loop(4, TILES, spread_step)
    wait_all(k_dp, kd_recv)
    k_full[...] = sum_slots(k_sum[...], k_dp, PEERS)
    start_all(kernel_gather)

    for i in range(ROWS):
        m = maskf[i : i + 1, :]
        grad_fields[i] = (m * (cot[i].astype(F32) + conv[i])).astype(BF16)

    even = core == 0
    for h in range(3):
        wait_all(lon_in.at[h], lon_recv.at[h])
        mine = dp_sum[h].astype(F32)
        other = lon_in[h, 1].astype(F32)
        for k in range(2, PEERS, 2):
            mine = mine + lon_in[h, k].astype(F32)
            other = other + lon_in[h, k + 1].astype(F32)
        totals[0, h] = jnp.where(even, mine, other)
        totals[1, h] = jnp.where(even, other, mine)
    wait_all(k_all, kg_recv)
    k_all[0] = k_full[...]
    for p in range(PEERS):
        kern_total[4 * p : 4 * p + 4, :] = k_all[lax.rem(lon - p + PEERS, PEERS)]
    for k in range(2):
        field_edge(k).wait_send()
        grad_edge(k).wait_send()
    for h in range(3):
        to_sibling(h).wait_send()
        wait_all(dp_in.at[h], dp_send.at[h])
        wait_all(lon_in.at[h], lon_send.at[h])
    wait_all(k_lon, ks_send)
    wait_all(k_dp, kd_send)
    wait_all(k_all, kg_send)
    store.wait()


def finish_kernel(
    out_in, grad_in, totals, kern_total,
    out, grad, g_in, g_out, g_gain, g_bias, g_kern,
    held, wide, tall, sems, *, scale
):
    steps = []
    for n in range(8):
        rows = pl.ds(4 * (n % 4), 4)
        src, dst = (out_in, out) if n < 4 else (grad_in, grad)
        steps.append(
            (
                pltpu.make_async_copy(src.at[rows], held.at[n], sems.at[0, n]),
                pltpu.make_async_copy(held.at[n], dst.at[rows], sems.at[1, n]),
            )
        )
    for load, _ in steps:
        load.start()
    for load, save in steps:
        load.wait()
        save.start()
    for h in range(3):
        turned = jnp.transpose(totals[0, h] * scale)
        for d in range(PEERS):
            tall[48 * d + 16 * h : 48 * d + 16 * h + 16, :] = turned[16 * d : 16 * d + 16, :]
        g_out[16 * h : 16 * h + 16, :] = totals[1, h, :, 0:CH] * scale
    wide[...] = jnp.transpose(tall[...])
    g_in[...] = wide[0:12, :]
    g_bias[...] = wide[12, :]
    g_gain[...] = kern_total[56:57, :] * scale
    for a in range(7):
        g_kern[a] = kern_total[8 * a : 8 * a + 7, :] * scale
    for _, save in steps:
        save.wait()


def vmem():
    return pl.BlockSpec(memory_space=pltpu.VMEM)


def anywhere():
    return pl.BlockSpec(memory_space=pl.ANY)


def per_device(fields, cotangent, land_sea, kernel, ln_gain, weight_in, bias_in, weight_out):
    x = jnp.transpose(fields, (0, 1, 3, 2)).reshape(ROWS, CH, LANES)
    cot = jnp.transpose(cotangent, (0, 1, 3, 2)).reshape(ROWS, CH, LANES)
    w_out_t = jnp.transpose(weight_out)
    dma = pltpu.SemaphoreType.DMA
    big = (ROWS, CH, LANES)
    wide = (STEPS, CH, STEP)
    piece = (4, CH)
    blk = (16, 256)

    out, grad_fields, totals, kern_total = pl.pallas_call(
        main_kernel,
        name="block_and_grads",
        out_shape=(
            jax.ShapeDtypeStruct(big, BF16),
            jax.ShapeDtypeStruct(big, BF16),
            jax.ShapeDtypeStruct((2, 3) + blk, F32),
            jax.ShapeDtypeStruct((64, CH), F32),
        ),
        in_specs=[vmem(), anywhere(), vmem(), vmem(), vmem(), anywhere(), vmem(), anywhere()],
        out_specs=(anywhere(), vmem(), vmem(), vmem()),
        scratch_shapes=[
            pltpu.VMEM(big, BF16),
            pltpu.VMEM((CH, HID), BF16),
            pltpu.VMEM((CH, HID), BF16),
            pltpu.VMEM(big, BF16),
            pltpu.VMEM(big, BF16),
            pltpu.VMEM(big, BF16),
            pltpu.VMEM(big, BF16),
            pltpu.VMEM(big, BF16),
            pltpu.VMEM(big, F32),
            pltpu.VMEM((3, STEPS, 256, STEP), BF16),
            pltpu.VMEM(wide, F32),
            pltpu.VMEM((LANES, CH), F32),
            pltpu.VMEM((CH, LANES), F32),
            pltpu.VMEM((56, CH, LANES), BF16),
            pltpu.VMEM((ROWS, 1, LANES), F32),
            pltpu.VMEM((CH, LANES), F32),
            pltpu.VMEM((3, 256, LANES), F32),
            pltpu.VMEM((3, 256, CH), BF16),
            pltpu.VMEM((3, CH, 256), BF16),
            pltpu.VMEM((3, 256, CH), BF16),
            pltpu.VMEM((3, CH, 256), BF16),
            pltpu.VMEM((STEPS, CH + 16, STEP), BF16),
            pltpu.VMEM(wide, BF16),
            pltpu.VMEM((ROWS, 1, LANES), F32),
            pltpu.VMEM((CH + 16, 256), F32),
            pltpu.VMEM((256, CH), F32),
            pltpu.VMEM((CH, LANES), F32),
            pltpu.VMEM(blk, F32),
            pltpu.VMEM((CH, LANES), BF16),
            pltpu.VMEM((2, CH, LANES), BF16),
            pltpu.VMEM((CH, LANES), BF16),
            pltpu.VMEM((2, CH, LANES), BF16),
            pltpu.VMEM((3, 2, PEERS) + blk, BF16),
            pltpu.VMEM((3, PEERS) + blk, BF16),
            pltpu.VMEM((3, PEERS) + blk, BF16),
            pltpu.VMEM((3, PEERS) + blk, BF16),
            pltpu.VMEM((3,) + blk, BF16),
            pltpu.VMEM((3, PEERS) + blk, BF16),
            pltpu.VMEM((PEERS,) + piece, F32),
            pltpu.VMEM((PEERS,) + piece, F32),
            pltpu.VMEM(piece, F32),
            pltpu.VMEM((PEERS,) + piece, F32),
            pltpu.VMEM(piece, F32),
            pltpu.VMEM((PEERS,) + piece, F32),
            dma((4,)),
            dma((2,)),
            dma((2,)),
            dma((2,)),
            dma((2,)),
            dma((3,)),
            dma((3,)),
            dma((3,)),
            dma((3,)),
            dma((3,)),
            dma((3,)),
            dma,
            dma,
            dma,
            dma,
            dma,
            dma,
        ],
        compiler_params=pltpu.CompilerParams(
            collective_id=0, has_side_effects=True, vmem_limit_bytes=VMEM_BYTES
        ),
    )(x, cot, land_sea, kernel, ln_gain.reshape(1, CH), weight_in, bias_in, w_out_t)

    total_cells = ROWS * LANES * lax.axis_size("dp") * lax.axis_size("lon")
    out, grad_fields, g_in, g_out, g_gain, g_bias, g_kern = pl.pallas_call(
        functools.partial(finish_kernel, scale=1.0 / math.sqrt(total_cells)),
        name="finish",
        out_shape=(
            jax.ShapeDtypeStruct(big, BF16),
            jax.ShapeDtypeStruct(big, BF16),
            jax.ShapeDtypeStruct((12, HID), F32),
            jax.ShapeDtypeStruct((48, CH), F32),
            jax.ShapeDtypeStruct((1, CH), F32),
            jax.ShapeDtypeStruct((HID,), F32),
            jax.ShapeDtypeStruct((7, 7, CH), F32),
        ),
        in_specs=[anywhere(), anywhere(), vmem(), vmem()],
        out_specs=(anywhere(), anywhere()) + (vmem(),) * 5,
        scratch_shapes=[
            pltpu.VMEM((8, 4, CH, LANES), BF16),
            pltpu.VMEM((16, HID), F32),
            pltpu.VMEM((HID, 16), F32),
            dma((2, 8)),
        ],
    )(out, grad_fields, totals, kern_total)

    def back(y):
        return jnp.transpose(y[None], (0, 1, 3, 2))

    return (
        back(out),
        back(grad_fields),
        g_in,
        g_out,
        g_kern,
        g_gain.reshape(CH),
        g_bias,
    )


def solution(mesh):
    placed = (
        P("dp", None, "lon", None),
        P("dp", None, "lon", None),
        P(None, "lon"),
        P(),
        P(),
        P(),
        P(),
        P(),
    )
    return jax.shard_map(
        per_device,
        mesh=mesh,
        in_specs=placed,
        out_specs=(
            P("dp", None, "lon", None),
            P("dp", None, "lon", None),
            P("dp", None),
            P("dp", None),
            P(),
            P(),
            P(),
        ),
        check_vma=False,
    )
```

```python
import functools
import math

import jax
import jax.numpy as jnp
from jax import lax
from jax.experimental import pallas as pl
from jax.experimental.pallas import tpu as pltpu
from jax.sharding import PartitionSpec as P

F32 = jnp.float32
BF16 = jnp.bfloat16
MESH = pl.DeviceIdType.MESH
ROWS = 16
CH = 192
HID = 768
LANES = 128
TILES = CH // 16
STEP = 1024
STEPS = ROWS * LANES // STEP
PEERS = 16
VMEM_BYTES = 60 * 1024 * 1024


def lane_ids(shape):
    return lax.broadcasted_iota(jnp.int32, shape, 1)


def pack_edges(row_of):
    group = ((lane_ids((CH, LANES)) + 4) // 8) % ROWS
    packed = jnp.zeros((CH, LANES), BF16)
    for i in range(ROWS):
        row = row_of(i)
        if i:
            row = pltpu.roll(row, 8 * i, axis=1)
        packed = jnp.where(group == i, row, packed)
    return packed


def merge_edges(from_left, from_right):
    return jnp.where(lane_ids((CH, LANES)) % 8 < 4, from_right, from_left)


def spread_edges(edges, halo_ref):
    for i in range(ROWS):
        halo_ref[i] = pltpu.roll(edges, (LANES - 8 * i) % LANES, axis=1) if i else edges


def shifted_rows(src, halo, c0, shift):
    lane = lane_ids((16, LANES))
    rows = []
    for r in range(ROWS):
        row = src[r, pl.ds(c0, 16), :]
        if shift > 0:
            row = jnp.where(lane < shift, halo[r, pl.ds(c0, 16), :], row)
        elif shift < 0:
            row = jnp.where(lane >= LANES + shift, halo[r, pl.ds(c0, 16), :], row)
        if shift:
            row = pltpu.roll(row, (LANES - shift) % LANES, axis=1)
        rows.append(row)
    return rows


def plus(total, term):
    return term if total is None else total + term


def conv_tile(src, halo, taps, dst, tile, sign):
    c0 = pl.multiple_of(tile * 16, 16)
    weights = taps[pl.ds(c0, 16), :]
    total = [None] * ROWS
    for b in range(7):
        rows = shifted_rows(src, halo, c0, sign * (b - 3))
        part = [None] * ROWS
        for a in range(7):
            col = 8 * a + b
            w = jnp.broadcast_to(weights[:, col : col + 1], (16, LANES)).astype(BF16)
            for i in range(ROWS):
                r = i + sign * (a - 3)
                if 0 <= r < ROWS:
                    part[i] = plus(part[i], w * rows[r])
        for i in range(ROWS):
            total[i] = plus(total[i], part[i].astype(F32))
    for i in range(ROWS):
        dst[i, pl.ds(c0, 16), :] = total[i]


def kernel_grad_tile(src, halo, grad, dst, tile):
    c0 = pl.multiple_of(tile * 16, 16)
    for b in range(7):
        rows = shifted_rows(src, halo, c0, b - 3)
        sums = [[None] * 7, [None] * 7]
        for i in range(ROWS):
            g = grad[i, pl.ds(c0, 16), :]
            part = sums[i // 8]
            for a in range(7):
                r = i + a - 3
                if 0 <= r < ROWS:
                    part[a] = plus(part[a], g * rows[r])
        for a in range(7):
            both = sums[0][a].astype(F32) + sums[1][a].astype(F32)
            dst[8 * a + b, pl.ds(c0, 16), :] = both.astype(BF16)


def sum_lanes(src):
    lane = lane_ids((LANES, LANES))
    total = jnp.zeros((CH, LANES), F32)
    for a in range(7):
        for b in range(7):
            pick = jnp.where(lane == 8 * a + b, 1.0, 0.0).astype(BF16)
            total = total + jnp.dot(src[8 * a + b], pick, preferred_element_type=F32)
    return total


def load_taps(kern_ref, stage, taps):
    stage[...] = jnp.zeros_like(stage)
    for a in range(7):
        stage[8 * a : 8 * a + 7, :] = kern_ref[a]
    taps[...] = jnp.transpose(stage[...])


def ring_neighbours():
    me = lax.axis_index("lon")
    return lax.rem(me + PEERS - 1, PEERS), lax.rem(me + 1, PEERS)


def lon_device(lon):
    return (lax.axis_index("dp"), lon)


def gelu_terms(z):
    half = 0.5 * (1.0 + lax.erf(z * (1.0 / math.sqrt(2.0))))
    slope = half + z * (jnp.exp(z * z * -0.5) * (1.0 / math.sqrt(2.0 * math.pi)))
    return z * half, slope


def loop(lo, hi, step):
    def body(t, carry):
        step(t)
        return carry

    lax.fori_loop(lo, hi, body, 0)


def main_kernel(
    fields, cot_hbm, mask, kern, gain_row, w_in_hbm, bias_row, w_out_t_hbm,
    out_hbm, grad_fields, totals, kern_total,
    cot, w_in_raw, w_out_t_raw, out,
    masked, m_halo, grad, d_halo, conv, acts, d_normed,
    stage, taps, tap_sums, m3, gain_col, bias_col,
    w_in_t, w_in, w_out, w_out_t, aug, gm, inv,
    part_in, part_out, gain_sum, block,
    m_edges, m_slots, d_edges, d_slots,
    parts, sib_in, half_sum, dp_in, dp_sum, lon_in,
    k_pieces, k_lon, k_sum, k_dp, k_full, k_all,
    load_sem, m_send, m_recv, d_send, d_recv, sib_send, sib_recv,
    dp_send, dp_recv, lon_send, lon_recv,
    ks_send, ks_recv, kd_send, kd_recv, kg_send, kg_recv,
):
    dp, lon = lax.axis_index("dp"), lax.axis_index("lon")
    left, right = ring_neighbours()
    core = lax.rem(lon, 2)
    sibling = lon + 1 - 2 * core
    barrier = pltpu.get_barrier_semaphore()

    def dp_peer(k):
        return (lax.rem(dp + k, PEERS), lon)

    def lon_peer(k):
        return (dp, lax.rem(lon + k, PEERS))

    def greet(k):
        pl.semaphore_signal(barrier, inc=1, device_id=dp_peer(k), device_id_type=MESH)
        pl.semaphore_signal(barrier, inc=1, device_id=lon_peer(k), device_id_type=MESH)

    def remote(src, dst, send, recv, device):
        return pltpu.make_async_remote_copy(
            src_ref=src, dst_ref=dst, send_sem=send, recv_sem=recv,
            device_id=device, device_id_type=MESH,
        )

    def field_edge(k):
        peer = (left, right)[k]
        return remote(m_edges, m_slots.at[k], m_send.at[k], m_recv.at[k], lon_device(peer))

    def grad_edge(k):
        peer = (left, right)[k]
        return remote(d_edges, d_slots.at[k], d_send.at[k], d_recv.at[k], lon_device(peer))

    def to_sibling(h):
        return remote(
            parts.at[h, 1 - core], sib_in.at[h], sib_send.at[h], sib_recv.at[h],
            lon_device(sibling),
        )

    def over_dp(h):
        def make(k):
            return remote(
                half_sum.at[h, lax.rem(dp + k, PEERS)], dp_in.at[h, k],
                dp_send.at[h], dp_recv.at[h], dp_peer(k),
            )

        return make

    def over_lon(h):
        def make(k):
            return remote(
                dp_sum.at[h], lon_in.at[h, k], lon_send.at[h], lon_recv.at[h], lon_peer(k)
            )

        return make

    def kernel_scatter(k):
        return remote(
            k_pieces.at[lax.rem(lon + k, PEERS)], k_lon.at[k], ks_send, ks_recv, lon_peer(k)
        )

    def kernel_over_dp(k):
        return remote(k_sum, k_dp.at[k], kd_send, kd_recv, dp_peer(k))

    def kernel_gather(k):
        return remote(k_full, k_all.at[k], kg_send, kg_recv, lon_peer(k))

    def start_all(make):
        loop(1, PEERS, lambda k: make(k).start())

    def wait_all(slots, sem):
        rows = slots.at[pl.ds(1, PEERS - 1)]
        pltpu.make_async_copy(rows, rows, sem).wait()

    def sum_slots(own, slots, count):
        def body(k, acc):
            return acc + slots[k].astype(F32)

        return lax.fori_loop(1, count, body, own.astype(F32))

    loads = [
        pltpu.make_async_copy(src, dst, load_sem.at[n])
        for n, (src, dst) in enumerate(
            ((w_in_hbm, w_in_raw), (w_out_t_hbm, w_out_t_raw), (cot_hbm, cot))
        )
    ]
    for load in loads:
        load.start()
    greet(1)
    greet(PEERS - 1)
    loop(2, PEERS - 1, greet)

    maskf = mask[...].astype(F32)
    for i in range(ROWS):
        m3[i] = maskf[i : i + 1, :]
        masked[i] = (fields[i].astype(F32) * maskf[i : i + 1, :]).astype(BF16)
    m_edges[...] = pack_edges(lambda i: masked[i])
    pl.semaphore_wait(barrier, 2 * (PEERS - 1))
    for k in range(2):
        field_edge(k).start()

    load_taps(kern, stage, taps)
    gain_col[...] = jnp.transpose(jnp.broadcast_to(gain_row[...], (LANES, CH)))
    bias_wide = jnp.transpose(jnp.broadcast_to(bias_row[...][None, :], (LANES, HID)))
    loads[0].wait()
    loads[1].wait()
    in_t = jnp.transpose(w_in_raw[...].astype(F32)).astype(BF16)
    out_n = jnp.transpose(w_out_t_raw[...].astype(F32)).astype(BF16)
    for h in range(3):
        for d in range(PEERS):
            to = slice(16 * d, 16 * d + 16)
            at = slice(48 * d + 16 * h, 48 * d + 16 * h + 16)
            w_in_t[h, to, :] = in_t[at, :]
            w_out[h, to, :] = out_n[at, :]
            bias_col[h, to, :] = bias_wide[at, :]
        w_in[h] = jnp.transpose(w_in_t[h].astype(F32)).astype(BF16)
        w_out_t[h] = jnp.transpose(w_out[h].astype(F32)).astype(BF16)
    ones_row = lax.broadcasted_iota(jnp.int32, (16, STEP), 0) == 0
    for k in range(STEPS):
        aug[k, CH : CH + 16, :] = jnp.where(ones_row, 1.0, 0.0).astype(BF16)
    gain_sum[...] = jnp.zeros_like(gain_sum)
    block[...] = jnp.zeros_like(block)
    loads[2].wait()
    per_step = STEP // LANES
    for i in range(ROWS):
        lanes = slice(LANES * (i % per_step), LANES * (i % per_step) + LANES)
        gm[i // per_step, :, lanes] = (cot[i].astype(F32) * m3[i]).astype(BF16)

    for k in range(2):
        field_edge(k).wait_recv()
    spread_edges(merge_edges(m_slots[1], m_slots[0]), m_halo)
    loop(0, TILES, lambda t: conv_tile(masked, m_halo, taps, conv, t, 1))
    def place(i):
        per = STEP // LANES
        return i // per, pl.ds(pl.multiple_of((i % per) * LANES, LANES), LANES)

    def by_four(step):
        def group(g):
            for u in range(4):
                step(4 * g + u)

        return group

    def norm_step(i):
        k, lanes = place(i)
        c = conv[i]
        mu = jnp.sum(c, axis=0, keepdims=True) * (1.0 / CH)
        centered = c - mu
        var = jnp.sum(centered * centered, axis=0, keepdims=True) * (1.0 / CH)
        inv_sigma = lax.rsqrt(var + 1e-6)
        nhat = centered * inv_sigma
        inv[i] = inv_sigma
        conv[i] = nhat
        aug[k, 0:CH, lanes] = (nhat * gain_col[...]).astype(BF16)

    loop(0, ROWS // 4, by_four(norm_step))

    def mlp_step(h, k):
        bias = jnp.concatenate([bias_col[h]] * (STEP // LANES), axis=1)
        pre = jnp.dot(w_in_t[h], aug[k, 0:CH, :], preferred_element_type=F32) + bias
        d_act = jnp.dot(w_out[h], gm[k], preferred_element_type=F32)
        act, slope = gelu_terms(pre)
        act = act.astype(BF16)
        d_pre = (d_act * slope).astype(BF16)
        acts[h, k] = act
        more_d = jnp.dot(w_in[h], d_pre, preferred_element_type=F32)
        if h == 0:
            d_normed[k] = more_d
        else:
            d_normed[k] += more_d
        more_in = lax.dot_general(
            aug[k], d_pre, (((1,), (1,)), ((), ())), preferred_element_type=F32
        )
        more_out = lax.dot_general(
            act, gm[k], (((1,), (1,)), ((), ())), preferred_element_type=F32
        )
        if k == 0:
            part_in[...] = more_in
            part_out[...] = more_out
        else:
            part_in[...] += more_in
            part_out[...] += more_out

    def exchange_half(h):
        to_sibling(h).wait_recv()

        def add(d):
            mine = parts[h, core, d].astype(F32)
            half_sum[h, d] = (mine + sib_in[h, d].astype(F32)).astype(BF16)

        loop(0, PEERS, add)
        start_all(over_dp(h))

    def exchange_sum(h):
        wait_all(dp_in.at[h], dp_recv.at[h])
        dp_sum[h] = sum_slots(half_sum[h, dp], dp_in.at[h], PEERS).astype(BF16)
        start_all(over_lon(h))

    for h in range(3):
        mlp_step(h, 0)
        if h:
            exchange_half(h - 1)
        mlp_step(h, 1)
        for d in range(PEERS):
            block[0:12, :] = part_in[12 * d : 12 * d + 12, :]
            block[12:13, :] = part_in[CH : CH + 1, :]
            parts[h, 0, d] = block[...].astype(BF16)
            parts[h, 1, d, :, 0:CH] = part_out[16 * d : 16 * d + 16, :].astype(BF16)
            parts[h, 1, d, :, CH:256] = jnp.zeros((16, 64), BF16)
        to_sibling(h).start()

    def norm_back(i):
        k, lanes = place(i)
        nhat = conv[i]
        d_n = d_normed[k, :, lanes]
        gain_sum[...] += d_n * nhat
        d_hat = d_n * gain_col[...]
        mean_d = jnp.sum(d_hat, axis=0, keepdims=True) * (1.0 / CH)
        mean_dn = jnp.sum(d_hat * nhat, axis=0, keepdims=True) * (1.0 / CH)
        grad[i] = (inv[i] * (d_hat - mean_d - nhat * mean_dn)).astype(BF16)

    loop(0, ROWS // 4, by_four(norm_back))
    exchange_half(2)
    d_edges[...] = pack_edges(lambda i: grad[i])
    for k in range(2):
        grad_edge(k).start()

    def kernel_step(t):
        kernel_grad_tile(masked, m_halo, grad, tap_sums, t)

    def spread_step(t):
        conv_tile(grad, d_halo, taps, conv, t, -1)

    def branch_step(k):
        branch = jnp.zeros((CH, STEP), F32)
        for h in range(3):
            branch = branch + jnp.dot(w_out_t[h], acts[h, k], preferred_element_type=F32)
        per = STEP // LANES
        for j in range(per):
            i = per * k + j
            kept = fields[i].astype(F32) + branch[:, LANES * j : LANES * j + LANES]
            out[i] = (m3[i] * kept).astype(BF16)

    loop(0, TILES, kernel_step)
    flipped = jnp.transpose(sum_lanes(tap_sums))
    gain_total = jnp.sum(jnp.transpose(gain_sum[...]), axis=0, keepdims=True)
    stage[0:64, :] = flipped[0:64, :]
    stage[56:57, :] = gain_total
    for p in range(PEERS):
        k_pieces[p] = stage[4 * p : 4 * p + 4, :]
    start_all(kernel_scatter)

    exchange_sum(0)
    branch_step(0)
    exchange_sum(1)
    branch_step(1)
    store = pltpu.make_async_copy(out, out_hbm, load_sem.at[3])
    store.start()
    for k in range(2):
        grad_edge(k).wait_recv()
    spread_edges(merge_edges(d_slots[1], d_slots[0]), d_halo)
    wait_all(k_lon, ks_recv)
    k_sum[...] = sum_slots(k_pieces[lon], k_lon, PEERS)
    start_all(kernel_over_dp)
    loop(0, 4, spread_step)
    exchange_sum(2)
    loop(4, TILES, spread_step)
    wait_all(k_dp, kd_recv)
    k_full[...] = sum_slots(k_sum[...], k_dp, PEERS)
    start_all(kernel_gather)

    for i in range(ROWS):
        m = maskf[i : i + 1, :]
        grad_fields[i] = (m * (cot[i].astype(F32) + conv[i])).astype(BF16)

    even = core == 0
    for h in range(3):
        wait_all(lon_in.at[h], lon_recv.at[h])
        mine = dp_sum[h].astype(F32)
        other = lon_in[h, 1].astype(F32)
        for k in range(2, PEERS, 2):
            mine = mine + lon_in[h, k].astype(F32)
            other = other + lon_in[h, k + 1].astype(F32)
        totals[0, h] = jnp.where(even, mine, other)
        totals[1, h] = jnp.where(even, other, mine)
    wait_all(k_all, kg_recv)
    k_all[0] = k_full[...]
    for p in range(PEERS):
        kern_total[4 * p : 4 * p + 4, :] = k_all[lax.rem(lon - p + PEERS, PEERS)]
    for k in range(2):
        field_edge(k).wait_send()
        grad_edge(k).wait_send()
    for h in range(3):
        to_sibling(h).wait_send()
        wait_all(dp_in.at[h], dp_send.at[h])
        wait_all(lon_in.at[h], lon_send.at[h])
    wait_all(k_lon, ks_send)
    wait_all(k_dp, kd_send)
    wait_all(k_all, kg_send)
    store.wait()


def finish_kernel(
    out_in, grad_in, totals, kern_total,
    out, grad, g_in, g_out, g_gain, g_bias, g_kern,
    held, wide, tall, sems, *, scale
):
    steps = []
    for n in range(8):
        rows = pl.ds(4 * (n % 4), 4)
        src, dst = (out_in, out) if n < 4 else (grad_in, grad)
        steps.append(
            (
                pltpu.make_async_copy(src.at[rows], held.at[n], sems.at[0, n]),
                pltpu.make_async_copy(held.at[n], dst.at[rows], sems.at[1, n]),
            )
        )
    for load, _ in steps:
        load.start()
    for load, save in steps:
        load.wait()
        save.start()
    for h in range(3):
        turned = jnp.transpose(totals[0, h] * scale)
        for d in range(PEERS):
            tall[48 * d + 16 * h : 48 * d + 16 * h + 16, :] = turned[16 * d : 16 * d + 16, :]
        g_out[16 * h : 16 * h + 16, :] = totals[1, h, :, 0:CH] * scale
    wide[...] = jnp.transpose(tall[...])
    g_in[...] = wide[0:12, :]
    g_bias[...] = wide[12, :]
    g_gain[...] = kern_total[56:57, :] * scale
    for a in range(7):
        g_kern[a] = kern_total[8 * a : 8 * a + 7, :] * scale
    for _, save in steps:
        save.wait()


def vmem():
    return pl.BlockSpec(memory_space=pltpu.VMEM)


def anywhere():
    return pl.BlockSpec(memory_space=pl.ANY)


def per_device(fields, cotangent, land_sea, kernel, ln_gain, weight_in, bias_in, weight_out):
    x = jnp.transpose(fields, (0, 1, 3, 2)).reshape(ROWS, CH, LANES)
    cot = jnp.transpose(cotangent, (0, 1, 3, 2)).reshape(ROWS, CH, LANES)
    w_out_t = jnp.transpose(weight_out)
    dma = pltpu.SemaphoreType.DMA
    big = (ROWS, CH, LANES)
    wide = (STEPS, CH, STEP)
    piece = (4, CH)
    blk = (16, 256)

    out, grad_fields, totals, kern_total = pl.pallas_call(
        main_kernel,
        name="block_and_grads",
        out_shape=(
            jax.ShapeDtypeStruct(big, BF16),
            jax.ShapeDtypeStruct(big, BF16),
            jax.ShapeDtypeStruct((2, 3) + blk, F32),
            jax.ShapeDtypeStruct((64, CH), F32),
        ),
        in_specs=[vmem(), anywhere(), vmem(), vmem(), vmem(), anywhere(), vmem(), anywhere()],
        out_specs=(anywhere(), vmem(), vmem(), vmem()),
        scratch_shapes=[
            pltpu.VMEM(big, BF16),
            pltpu.VMEM((CH, HID), BF16),
            pltpu.VMEM((CH, HID), BF16),
            pltpu.VMEM(big, BF16),
            pltpu.VMEM(big, BF16),
            pltpu.VMEM(big, BF16),
            pltpu.VMEM(big, BF16),
            pltpu.VMEM(big, BF16),
            pltpu.VMEM(big, F32),
            pltpu.VMEM((3, STEPS, 256, STEP), BF16),
            pltpu.VMEM(wide, F32),
            pltpu.VMEM((LANES, CH), F32),
            pltpu.VMEM((CH, LANES), F32),
            pltpu.VMEM((56, CH, LANES), BF16),
            pltpu.VMEM((ROWS, 1, LANES), F32),
            pltpu.VMEM((CH, LANES), F32),
            pltpu.VMEM((3, 256, LANES), F32),
            pltpu.VMEM((3, 256, CH), BF16),
            pltpu.VMEM((3, CH, 256), BF16),
            pltpu.VMEM((3, 256, CH), BF16),
            pltpu.VMEM((3, CH, 256), BF16),
            pltpu.VMEM((STEPS, CH + 16, STEP), BF16),
            pltpu.VMEM(wide, BF16),
            pltpu.VMEM((ROWS, 1, LANES), F32),
            pltpu.VMEM((CH + 16, 256), F32),
            pltpu.VMEM((256, CH), F32),
            pltpu.VMEM((CH, LANES), F32),
            pltpu.VMEM(blk, F32),
            pltpu.VMEM((CH, LANES), BF16),
            pltpu.VMEM((2, CH, LANES), BF16),
            pltpu.VMEM((CH, LANES), BF16),
            pltpu.VMEM((2, CH, LANES), BF16),
            pltpu.VMEM((3, 2, PEERS) + blk, BF16),
            pltpu.VMEM((3, PEERS) + blk, BF16),
            pltpu.VMEM((3, PEERS) + blk, BF16),
            pltpu.VMEM((3, PEERS) + blk, BF16),
            pltpu.VMEM((3,) + blk, BF16),
            pltpu.VMEM((3, PEERS) + blk, BF16),
            pltpu.VMEM((PEERS,) + piece, F32),
            pltpu.VMEM((PEERS,) + piece, F32),
            pltpu.VMEM(piece, F32),
            pltpu.VMEM((PEERS,) + piece, F32),
            pltpu.VMEM(piece, F32),
            pltpu.VMEM((PEERS,) + piece, F32),
            dma((4,)),
            dma((2,)),
            dma((2,)),
            dma((2,)),
            dma((2,)),
            dma((3,)),
            dma((3,)),
            dma((3,)),
            dma((3,)),
            dma((3,)),
            dma((3,)),
            dma,
            dma,
            dma,
            dma,
            dma,
            dma,
        ],
        compiler_params=pltpu.CompilerParams(
            collective_id=0, has_side_effects=True, vmem_limit_bytes=VMEM_BYTES
        ),
    )(x, cot, land_sea, kernel, ln_gain.reshape(1, CH), weight_in, bias_in, w_out_t)

    total_cells = ROWS * LANES * lax.axis_size("dp") * lax.axis_size("lon")
    out, grad_fields, g_in, g_out, g_gain, g_bias, g_kern = pl.pallas_call(
        functools.partial(finish_kernel, scale=1.0 / math.sqrt(total_cells)),
        name="finish",
        out_shape=(
            jax.ShapeDtypeStruct(big, BF16),
            jax.ShapeDtypeStruct(big, BF16),
            jax.ShapeDtypeStruct((12, HID), F32),
            jax.ShapeDtypeStruct((48, CH), F32),
            jax.ShapeDtypeStruct((1, CH), F32),
            jax.ShapeDtypeStruct((HID,), F32),
            jax.ShapeDtypeStruct((7, 7, CH), F32),
        ),
        in_specs=[anywhere(), anywhere(), vmem(), vmem()],
        out_specs=(anywhere(), anywhere()) + (vmem(),) * 5,
        scratch_shapes=[
            pltpu.VMEM((8, 4, CH, LANES), BF16),
            pltpu.VMEM((16, HID), F32),
            pltpu.VMEM((HID, 16), F32),
            dma((2, 8)),
        ],
    )(out, grad_fields, totals, kern_total)

    def back(y):
        return jnp.transpose(y[None], (0, 1, 3, 2))

    return (
        back(out),
        back(grad_fields),
        g_in,
        g_out,
        g_kern,
        g_gain.reshape(CH),
        g_bias,
    )


def solution(mesh):
    placed = (
        P("dp", None, "lon", None),
        P("dp", None, "lon", None),
        P(None, "lon"),
        P(),
        P(),
        P(),
        P(),
        P(),
    )
    return jax.shard_map(
        per_device,
        mesh=mesh,
        in_specs=placed,
        out_specs=(
            P("dp", None, "lon", None),
            P("dp", None, "lon", None),
            P("dp", None),
            P("dp", None),
            P(),
            P(),
            P(),
        ),
        check_vma=False,
    )
```
